128 devices in a mesh: comp: 16 (over y, x), port: 8 (over z, core).
Axes of the slice: x: 4, y: 4, z: 4, core: 2. Of those that a mesh axis runs over, the one named last changes fastest.
Arguments:
- mode_shapes: bfloat16 [256, 8192, 128], P('comp', 'port'), may hold values from -0.0625 to 0.0625
- block_values: bfloat16 [256, 64, 3, 128, 128], P('comp', 'port'), may hold values from -1.1953125 to 1.1953125
- block_offsets: int32 [256, 64, 3], P('comp', 'port'), may hold values from -2 to 2
- conductance: float32 [256, 8192], P('comp', 'port'), may hold values from 0.1 to 10
- capacity: float32 [256, 8192], P('comp', 'port'), may hold values from 0.1 to 10
- coupling: bfloat16 [256, 4, 128, 256], P('comp'), may hold values from -384 to 384
- surface_blocks: int32 [256, 4], P('comp'), may hold values from 0 to 63, as said below
- port_ids: int32 [256, 4], P('comp'), may hold values from 0 to 255, as said below
- port_counts: int32 [256], P('comp'), may hold values from 1 to 4
- boundary: float32 [256, 256, 256], P(('comp', 'port')), may hold values from -3 to 3
Outputs:
- modal_conductance: float32 [256, 128, 128], P('comp', 'port')
- modal_capacity: float32 [256, 128, 128], P('comp', 'port')
- interface: float32 [256, 256, 256], P(('comp', 'port'))
The draws below stay inside these ranges and needn't reach their ends.
Inputs may be any that keep to these rules, and one draw needn't show every extreme that they name: Slot s of component c has its surface cells on index surface_blocks[c, s] // 8 of port; its port is owned on index (port_ids[c, s] // 2) % 8 of port. Among the slots of the components of one index of comp, padding slots included, at most 2 lie on one index of port and name ports owned on one given index of port, and in every index of comp one such pair holds exactly 2. `port_ids`: port p is stored on device p // 2 of comp+port. Among the slots of the components of one index of comp, padding slots included, at most 2 name ports stored on one given device, and in every index of comp some device receives exactly 2; see surface_blocks for the other bound.
All inputs are finite; a program needn't handle non-finite values.
Results may differ from the reference program's by a relative error of at most 0.0008.
Values may be sent and summed in bfloat16 or wider, within the bound.
A program may use at most 320 MiB of HBM per device.

```python
import math
import jax
import jax.numpy as jnp
from jax import lax

M = 128
PB = 256
BS = 128
NB = 3
NP = 4
CD = 16
NBL = 8
PORT_DEV = 2
C = 256
NBR = 64
NI = 8192
P_SIZE = 256
CAP = 2
OWN_CAP = 2
N_COMP = 16
N_PORT = 8


def joint_draw(key):
    length = CD * NP
    whole = N_PORT * N_PORT * CAP

    def one_block(block_key):
        keys = jax.random.split(block_key, 6)
        hottest = jax.random.randint(keys[0], (), 0, N_PORT * N_PORT)
        others = jax.random.permutation(keys[1], whole - CAP)
        others = jnp.where(others >= hottest * CAP, others + CAP, others)
        sequence = jnp.concatenate([hottest * CAP + jnp.arange(CAP, dtype=jnp.int32), others[:length - CAP].astype(jnp.int32)])
        shuffle = jax.random.permutation(keys[2], length)
        sequence = sequence[shuffle]
        cell_id = sequence // CAP
        shard_of = cell_id // N_PORT
        owner_port = cell_id % N_PORT
        surface = shard_of * NBL + jax.random.randint(keys[3], (length,), 0, NBL)
        order = jnp.arange(length, dtype=jnp.int32)
        earlier = (owner_port[:, None] == owner_port[None, :]) & (order[:, None] > order[None, :])
        rank_in = jnp.sum(earlier.astype(jnp.int32), axis=1)
        tables = jax.vmap(lambda table_key: jax.random.permutation(table_key, N_COMP).astype(jnp.int32))(jax.random.split(keys[4], N_PORT))
        comp_target = tables[owner_port, rank_in // OWN_CAP]
        remainder = jax.random.randint(keys[5], (length,), 0, PORT_DEV)
        ports = (comp_target * N_PORT + owner_port) * PORT_DEV + remainder
        return (surface.reshape(CD, NP).astype(jnp.int32), ports.reshape(CD, NP).astype(jnp.int32))
    block_keys = jax.random.split(jax.random.fold_in(key, 7), N_COMP)
    surfaces, ports = jax.vmap(one_block)(block_keys)
    return (surfaces.reshape(C, NP), ports.reshape(C, NP))


def draw_surface_blocks(key, part):
    surfaces, ports = joint_draw(key)
    return surfaces


def draw_port_ids(key, part):
    surfaces, ports = joint_draw(key)
    return ports


def draw_coupling(key, part):
    spread = math.sqrt(NBR / 2.0)
    keys = jax.random.split(jax.random.fold_in(key, 11), 2)
    shared = 0.3
    single = jax.random.truncated_normal(keys[0], -4.0, 4.0, (C, NP, BS, PB), jnp.float32)
    common = jax.random.truncated_normal(keys[1], -4.0, 4.0, (C, NP, BS, 1), jnp.float32)
    mixed = math.sqrt(1.0 - shared) * single + math.sqrt(shared) * common
    return (spread * mixed).astype(jnp.bfloat16)


def place_ends(result, rng, smallest, high):
    shape = result.shape
    place = [jax.random.randint(jax.random.fold_in(rng, axis), (), 0, shape[axis]) for axis in range(len(shape))]
    result = result.at[tuple(place)].set(smallest)
    longest = shape.index(max(shape))
    place[longest] = (place[longest] + 1) % shape[longest]
    return result.at[tuple(place)].set(high)


def shard_levels(stream_key, dims, shards, smallest, high):
    factor_of = 1.0
    for position, shards_of in shards:
        heights = jax.random.uniform(jax.random.fold_in(jax.random.fold_in(stream_key, 6), position), (shards_of,), jnp.float32, smallest / len(shards), high / len(shards))
        factor_of = factor_of * jnp.repeat(jnp.exp(heights), dims[position] // shards_of).reshape((-1,) + (1,) * (len(dims) - 1 - position))
    return factor_of


def normal_values(key, dims, deviation, reach, shards=(), held_as=jnp.bfloat16):
    entries = jax.random.normal(key, dims, jnp.float32) * deviation
    if len(shards) > 0:
        entries = shard_levels(key, dims, shards, -0.22, 0.18) * entries
    return jnp.clip(entries, min=-reach, max=reach).astype(held_as)


def setup_inputs(seed: int = 0) -> dict:
    seeds = jax.random.split(jax.random.key(seed), 11)
    mode_shapes = normal_values(seeds[0], (C, NI, M), NI ** -0.5, 0.0625, ((0, 16), (1, 8)))
    block_values = normal_values(seeds[1], (C, NBR, NB, BS, BS), 0.2, 1.1953125, ((0, 16), (1, 8)))
    block_offsets = place_ends(jax.random.randint(seeds[2], (C, NBR, NB), -2, 3), jax.random.fold_in(seeds[2], 1), -2, 2).astype(jnp.int32)
    conductance = jnp.clip(jnp.exp(math.log(10.0) - 4.6051702 * jax.random.uniform(seeds[3], (C, NI), jnp.float32) ** shard_levels(seeds[3], (C, NI), ((0, 16), (1, 8)), -0.2, 0.2)), 0.1, 10.0)
    capacity = jnp.clip(jnp.exp(math.log(10.0) - 4.6051702 * jax.random.uniform(seeds[4], (C, NI), jnp.float32) ** shard_levels(seeds[4], (C, NI), ((0, 16), (1, 8)), -0.2, 0.2)), 0.1, 10.0)
    coupling = draw_coupling(jax.random.fold_in(seeds[10], 71), 0)
    surface_blocks = draw_surface_blocks(jax.random.fold_in(seeds[10], 71), 0)
    port_ids = draw_port_ids(jax.random.fold_in(seeds[10], 71), 0)
    port_counts = place_ends(jax.random.randint(seeds[8], (C,), 1, NP + 1), jax.random.fold_in(seeds[8], 1), 1, NP).astype(jnp.int32)
    boundary = normal_values(seeds[9], (P_SIZE, PB, PB), 0.5, 3.0, ((0, 128),), jnp.float32)
    return {"mode_shapes": mode_shapes, "block_values": block_values, "block_offsets": block_offsets, "conductance": conductance, "capacity": capacity, "coupling": coupling, "surface_blocks": surface_blocks, "port_ids": port_ids, "port_counts": port_counts, "boundary": boundary}


def reference(mode_shapes, block_values, block_offsets, conductance, capacity, coupling, surface_blocks, port_ids, port_counts, boundary):
    def modal(packed):
        shapes_one, values_one, offsets_one, conduct_one, capacity_one = packed
        shaped = shapes_one.reshape(NBR, BS, M)
        margin = jnp.zeros((2, BS, M), shapes_one.dtype)
        padded = jnp.concatenate([margin, shaped, margin], axis=0)
        rows_at = jnp.arange(NBR, dtype=jnp.int32)[:, None] + offsets_one.astype(jnp.int32) + 2
        summed = conduct_one[:, None] * shapes_one.astype(jnp.float32)
        for stored in range(NB):
            fetched = padded[rows_at[:, stored]]
            product = jnp.einsum("rij,rjm->rim", values_one[:, stored].astype(jnp.float32), fetched.astype(jnp.float32))
            summed = summed + product.reshape(NI, M)
        conducted = summed.astype(jnp.bfloat16)
        weighted = (capacity_one[:, None] * shapes_one.astype(jnp.float32)).astype(jnp.bfloat16)
        first = jnp.dot(shapes_one.T, conducted, preferred_element_type=jnp.float32)
        second = jnp.dot(shapes_one.T, weighted, preferred_element_type=jnp.float32)
        return first, second

    modal_conductance, modal_capacity = lax.map(modal, (mode_shapes, block_values, block_offsets, conductance, capacity))

    def assemble(summed, packed):
        shapes_one, couple_one, surface_one, ports_one, count_one = packed
        rows = shapes_one.reshape(NBR, BS, M)[surface_one]
        factors = jnp.einsum("sbm,sbp->smp", rows.astype(jnp.float32), couple_one.astype(jnp.float32)).astype(jnp.bfloat16)
        live = (jnp.arange(NP, dtype=jnp.int32) < count_one).astype(jnp.float32)
        wide = factors.astype(jnp.float32)
        squares = jnp.einsum("smp,smq->spq", wide, wide) * (1.0 / M)
        squares = squares * live[:, None, None]
        return summed.at[ports_one].add(squares), None

    interface, unused = lax.scan(assemble, boundary, (mode_shapes, coupling, surface_blocks, port_ids, port_counts))
    return modal_conductance, modal_capacity, interface
```

```python
import jax
import jax.numpy as jnp
from jax import lax
from jax.experimental import pallas as pl
from jax.experimental.pallas import tpu as pltpu
from jax.sharding import PartitionSpec as P

BF, F32, I32 = jnp.bfloat16, jnp.float32, jnp.int32
COMPS, PORTS = 16, 8
CD, NBL, NB, NP = 16, 8, 3, 4
BS, M, PB = 128, 128, 256
TOP = COMPS * 8


def nt(a, b):
    return lax.dot_general(a, b, (((1,), (1,)), ((), ())), preferred_element_type=F32)


def tn(a, b):
    return lax.dot_general(a, b, (((0,), (0,)), ((), ())), preferred_element_type=F32)


def remote(src, dst, send, recv, **where):
    return pltpu.make_async_remote_copy(
        src_ref=src,
        dst_ref=dst,
        send_sem=send,
        recv_sem=recv,
        device_id=where,
        device_id_type=pl.DeviceIdType.MESH,
    )


def fill_tables(me_port, ports_s, surface_s, ports_v, surface_v, counts_v, table):
    ports, surface = ports_v[...], surface_v[...]
    owner, target = (ports >> 1) & 7, ports >> 4
    shard = surface >> 3
    cell, device = shard * 8 + owner, ports >> 1
    comp = lax.broadcasted_iota(I32, (NP, CD), 1)
    slot = lax.broadcasted_iota(I32, (NP, CD), 0)
    order = comp * NP + slot
    alive = slot < counts_v[...]

    def count(c, ranks):
        in_cell, in_device = ranks
        for s in range(NP):
            port, block, at = ports_s[s, c], surface_s[s, c], c * NP + s
            this_device = port >> 1
            this_cell = (block >> 3) * 8 + (this_device & 7)
            later = order > at
            in_cell += jnp.where(later & (cell == this_cell), 1, 0)
            in_device += jnp.where(later & (device == this_device), 1, 0)
        return in_cell, in_device

    zero = jnp.zeros((NP, CD), I32)
    in_cell, in_device = lax.fori_loop(0, CD, count, (zero, zero))
    code = 2048 + (ports & 1) * 1024 + (shard * 2 + in_cell) * 64 + order
    here = alive & (owner == me_port)
    code = jnp.where(here, code, 0)
    device_key = target * 2 + in_device
    row = comp * NBL + (surface & 7)
    cell_key = jnp.where(shard == me_port, owner * 2 + in_cell, -1)
    q = lax.broadcasted_iota(I32, (TOP, CD), 0)
    wanted = (q >> 3) * 2 + (q & 1)
    total = jnp.zeros((TOP, CD), I32)
    for s in range(NP):
        total += jnp.where(device_key[s : s + 1] == wanted, code[s : s + 1], 0)
    table[0:TOP] = jnp.broadcast_to(jnp.sum(total, axis=1, keepdims=True), (TOP, 128))
    wanted = lax.broadcasted_iota(I32, (16, CD), 0)
    total = jnp.zeros((16, CD), I32)
    for s in range(NP):
        total += jnp.where(cell_key[s : s + 1] == wanted, row[s : s + 1], 0)
    table[TOP : TOP + 16] = jnp.broadcast_to(jnp.sum(total, axis=1, keepdims=True), (16, 128))


def kernel(
    offs,
    ports_s,
    surface_s,
    ports_v,
    surface_v,
    counts_v,
    shapes,
    values,
    cond_hbm,
    cap_hbm,
    coupling,
    boundary,
    cond_out,
    cap_out,
    face_out,
    phi,
    vals,
    coup,
    cond,
    cap,
    bound,
    table,
    table_s,
    codes,
    codes_s,
    rows_out,
    rows_in,
    halo_lo,
    halo_hi,
    win,
    scaled,
    part,
    pair_in,
    zsum,
    z_in,
    fac_out,
    fac_in,
    acc,
    load_sem,
    vals_sem,
    rows_ss,
    rows_rs,
    halo_ss,
    halo_rs,
    pair_ss,
    pair_rs,
    z_ss,
    z_rs,
    fac_ss,
    fac_rs,
    code_ss,
    code_rs,
):
    c_me, p_me = lax.axis_index("comp"), lax.axis_index("port")
    y, x = c_me // 4, c_me % 4
    z, core = p_me // 2, p_me % 2
    before, after = (p_me + PORTS - 1) % PORTS, (p_me + 1) % PORTS

    def to_comp(j):
        return ((y + j // 4) % 4) * 4 + (x + j % 4) % 4

    def from_comp(j):
        return ((y + 4 - j // 4) % 4) * 4 + (x + 4 - j % 4) % 4

    barrier = pltpu.get_barrier_semaphore()

    @pl.loop(1, PORTS)
    def _(j):
        pl.semaphore_signal(barrier, 1, device_id={"port": (p_me + j) % PORTS}, device_id_type=pl.DeviceIdType.MESH)

    @pl.loop(1, COMPS)
    def _(j):
        pl.semaphore_signal(barrier, 1, device_id={"comp": to_comp(j)}, device_id_type=pl.DeviceIdType.MESH)

    load_phi = pltpu.make_async_copy(shapes, phi, load_sem.at[0])
    load_coup = pltpu.make_async_copy(coupling, coup, load_sem.at[1])
    load_cond = pltpu.make_async_copy(cond_hbm, cond, load_sem.at[2])
    load_cap = pltpu.make_async_copy(cap_hbm, cap, load_sem.at[3])
    load_bound = pltpu.make_async_copy(boundary, bound, load_sem.at[4])
    load_phi.start()
    load_coup.start()
    load_cond.start()
    load_cap.start()

    def load_vals(c):
        return pltpu.make_async_copy(values.at[c], vals.at[c], vals_sem.at[c])

    @pl.loop(0, CD)
    def _(c):
        load_vals(c).start()

    load_bound.start()
    fill_tables(p_me, ports_s, surface_s, ports_v, surface_v, counts_v, table)
    to_smem = pltpu.make_async_copy(table, table_s, load_sem.at[5])
    to_smem.start()
    load_phi.wait()
    to_smem.wait()

    @pl.loop(0, PORTS)
    def _(o):
        for k in range(2):
            picked = table_s[TOP + 2 * o + k, 0]
            rows_out[o, k] = phi[picked].T

    rows_in[p_me] = rows_out[p_me]
    codes[pl.ds(pl.multiple_of(c_me * 8, 8), 8)] = table[pl.ds(pl.multiple_of(c_me * 8, 8), 8)]
    pl.semaphore_wait(barrier, PORTS - 1 + COMPS - 1)

    def send_rows(j):
        o = (p_me + j) % PORTS
        return remote(rows_out.at[o], rows_in.at[p_me], rows_ss.at[o], rows_rs.at[p_me], port=o)

    def recv_rows(j):
        o = (p_me + PORTS - j) % PORTS
        return remote(rows_out.at[o], rows_in.at[o], rows_ss.at[o], rows_rs.at[o], port=o)

    @pl.loop(1, PORTS)
    def _(j):
        send_rows(j).start()

    def send_up(c):
        return remote(
            shapes.at[pl.ds(c * NBL + NBL - 2, 2)], halo_lo.at[c], halo_ss.at[0, c], halo_rs.at[0, c], port=after
        )

    def send_down(c):
        return remote(shapes.at[pl.ds(c * NBL, 2)], halo_hi.at[c], halo_ss.at[1, c], halo_rs.at[1, c], port=before)

    @pl.loop(0, CD)
    def _(c):
        send_up(c).start()
        send_down(c).start()

    def send_codes(j):
        d = to_comp(j)
        return remote(
            table.at[pl.ds(pl.multiple_of(d * 8, 8), 8)],
            codes.at[pl.ds(pl.multiple_of(c_me * 8, 8), 8)],
            code_ss.at[d],
            code_rs.at[c_me],
            comp=d,
        )

    def recv_codes(j):
        d = from_comp(j)
        return remote(
            table.at[pl.ds(pl.multiple_of(d * 8, 8), 8)],
            codes.at[pl.ds(pl.multiple_of(d * 8, 8), 8)],
            code_ss.at[d],
            code_rs.at[d],
            comp=d,
        )

    @pl.loop(1, COMPS)
    def _(j):
        send_codes(j).start()

    load_coup.wait()

    @pl.loop(1, PORTS)
    def _(j):
        recv_rows(j).wait_recv()

    def factor(d, k):
        code = table_s[d * 8 + k, 0]
        rows = rows_in[(code >> 7) & 7, (code >> 6) & 1]
        return jnp.dot(rows, coup[code & 63], preferred_element_type=F32).astype(BF)

    def send_factors(j):
        d = to_comp(j)
        return remote(fac_out.at[d], fac_in.at[c_me], fac_ss.at[d], fac_rs.at[c_me], comp=d)

    def recv_factors(j):
        d = from_comp(j)
        return remote(fac_out.at[d], fac_in.at[d], fac_ss.at[d], fac_rs.at[d], comp=d)

    @pl.loop(1, COMPS)
    def _(j):
        d = to_comp(j)
        for k in range(2):
            fac_out[d, pl.ds(k * M, M)] = factor(d, k)
        send_factors(j).start()

    for k in range(2):
        fac_in[c_me, pl.ds(k * M, M)] = factor(c_me, k)

    def send_pair(c):
        return remote(
            part.at[1 - core, :, c], pair_in.at[:, c], pair_ss.at[c], pair_rs.at[c], port=2 * z + 1 - core
        )

    def send_z(d, h):
        to = (z + d) % 4
        return remote(
            zsum.at[to, pl.ds(2 * h, 2)], z_in.at[z, pl.ds(2 * h, 2)], z_ss.at[to, h], z_rs.at[z, h], port=2 * to + core
        )

    def recv_z(d, h):
        at = (z + 4 - d) % 4
        return remote(
            zsum.at[at, pl.ds(2 * h, 2)], z_in.at[at, pl.ds(2 * h, 2)], z_ss.at[at, h], z_rs.at[at, h], port=2 * at + core
        )

    def chip_sums(h):
        for i in range(2):
            c = 2 * h + i
            send_pair(c).wait_recv()
            zsum[:, c] = part[core, :, c] + pair_in[:, c]
        for d in range(1, 4):
            send_z(d, h).start()

    first = jnp.where(p_me == 0, 0.0, 1.0)
    last = jnp.where(p_me == PORTS - 1, 0.0, 1.0)

    def modal(c):
        load_vals(c).wait()
        send_up(c).wait_recv()
        send_down(c).wait_recv()
        for i in range(2):
            win[i] = (halo_lo[c, i].astype(F32) * first).T.astype(BF)
            win[NBL + 2 + i] = (halo_hi[c, i].astype(F32) * last).T.astype(BF)
        for r in range(NBL):
            win[2 + r] = phi[c * NBL + r].T
        base = pl.multiple_of((c // 8) * 8, 8)
        mine = lax.broadcasted_iota(I32, (8, NBL * BS), 0) == c % 8
        cond_row = jnp.sum(jnp.where(mine, cond[pl.ds(base, 8)], 0.0), axis=0, keepdims=True)
        cap_row = jnp.sum(jnp.where(mine, cap[pl.ds(base, 8)], 0.0), axis=0, keepdims=True)
        for r in range(NBL):
            cells = slice(r * BS, (r + 1) * BS)
            near = jnp.concatenate([win[r + 2 + offs[k, r, c]] for k in range(NB)], axis=1)
            blocks = jnp.concatenate([vals[c, r, k] for k in range(NB)], axis=1)
            own = win[r + 2].astype(F32)
            scaled[0:M, cells] = (nt(near, blocks) + cond_row[:, cells] * own).astype(BF)
            scaled[M : 2 * M, cells] = (cap_row[:, cells] * own).astype(BF)
        every = jnp.concatenate([win[r + 2] for r in range(NBL)], axis=1)
        sums = nt(every, scaled[...])
        for p in range(PORTS):
            part[p % 2, p // 2, c] = sums[16 * p : 16 * p + 16]

    load_cond.wait()
    load_cap.wait()

    @pl.loop(0, CD // 2)
    def _(h):
        @pl.loop(0, 2)
        def _(i):
            modal(2 * h + i)
            send_pair(2 * h + i).start()

        @pl.when(h > 0)
        def _():
            chip_sums(h - 1)

    chip_sums(CD // 2 - 1)

    @pl.loop(1, COMPS)
    def _(j):
        recv_codes(j).wait_recv()

    to_smem = pltpu.make_async_copy(codes, codes_s, load_sem.at[6])
    to_smem.start()
    acc[...] = jnp.zeros_like(acc)
    to_smem.wait()

    def square(d):
        for o in range(2):
            halves = []
            for k in range(2):
                code = codes_s[d * 8 + k, 0]
                weight = jnp.where((code >> 10) == 2 + o, 1.0, 0.0).astype(F32)
                halves.append((fac_in[d, pl.ds(k * M, M)].astype(F32) * weight).astype(BF))
            acc[o] += tn(jnp.concatenate(halves, axis=0), fac_in[d])

    square(c_me)

    @pl.loop(1, COMPS)
    def _(j):
        recv_factors(j).wait_recv()
        square(from_comp(j))

    load_bound.wait()
    face_out[...] = bound[...] + acc[...] * (1.0 / M)

    @pl.loop(0, CD // 2)
    def _(h):
        for d in range(1, 4):
            recv_z(d, h).wait_recv()
        for i in range(2):
            c = 2 * h + i
            total = zsum[z, c]
            for d in range(1, 4):
                total = total + z_in[(z + 4 - d) % 4, c]
            cond_out[c] = total[:, 0:M]
            cap_out[c] = total[:, M : 2 * M]
        for d in range(1, 4):
            send_z(d, h).wait_send()

    @pl.loop(0, CD)
    def _(c):
        send_up(c).wait_send()
        send_down(c).wait_send()
        send_pair(c).wait_send()

    @pl.loop(1, PORTS)
    def _(j):
        send_rows(j).wait_send()

    @pl.loop(1, COMPS)
    def _(j):
        send_factors(j).wait_send()
        send_codes(j).wait_send()


def shards(
    mode_shapes,
    block_values,
    block_offsets,
    conductance,
    capacity,
    coupling,
    surface_blocks,
    port_ids,
    port_counts,
    boundary,
):
    smem = pl.BlockSpec(memory_space=pltpu.SMEM)
    vmem = pl.BlockSpec(memory_space=pltpu.VMEM)
    hbm = pl.BlockSpec(memory_space=pl.ANY)
    dma = pltpu.SemaphoreType.DMA
    ports, surface = port_ids.T, surface_blocks.T
    return pl.pallas_call(
        kernel,
        out_shape=(
            jax.ShapeDtypeStruct((CD, M // PORTS, M), F32),
            jax.ShapeDtypeStruct((CD, M // PORTS, M), F32),
            jax.ShapeDtypeStruct((2, PB, PB), F32),
        ),
        in_specs=[smem] * 3 + [vmem] * 3 + [hbm] * 6,
        out_specs=(vmem, vmem, vmem),
        scratch_shapes=[
            pltpu.VMEM((CD * NBL, BS, M), BF),
            pltpu.VMEM((CD, NBL, NB, BS, BS), BF),
            pltpu.VMEM((CD * NP, BS, PB), BF),
            pltpu.VMEM((CD, NBL * BS), F32),
            pltpu.VMEM((CD, NBL * BS), F32),
            pltpu.VMEM((2, PB, PB), F32),
            pltpu.VMEM((TOP + 16, 128), I32),
            pltpu.SMEM((TOP + 16, 128), I32),
            pltpu.VMEM((TOP, 128), I32),
            pltpu.SMEM((TOP, 128), I32),
            pltpu.VMEM((PORTS, 2, M, BS), BF),
            pltpu.VMEM((PORTS, 2, M, BS), BF),
            pltpu.VMEM((CD, 2, BS, M), BF),
            pltpu.VMEM((CD, 2, BS, M), BF),
            pltpu.VMEM((NBL + 4, M, BS), BF),
            pltpu.VMEM((2 * M, NBL * BS), BF),
            pltpu.VMEM((2, 4, CD, 16, 2 * M), F32),
            pltpu.VMEM((4, CD, 16, 2 * M), F32),
            pltpu.VMEM((4, CD, 16, 2 * M), F32),
            pltpu.VMEM((4, CD, 16, 2 * M), F32),
            pltpu.VMEM((COMPS, 2 * M, PB), BF),
            pltpu.VMEM((COMPS, 2 * M, PB), BF),
            pltpu.VMEM((2, PB, PB), F32),
            dma((7,)),
            dma((CD,)),
            dma((PORTS,)),
            dma((PORTS,)),
            dma((2, CD)),
            dma((2, CD)),
            dma((CD,)),
            dma((CD,)),
            dma((4, CD // 2)),
            dma((4, CD // 2)),
            dma((COMPS,)),
            dma((COMPS,)),
            dma((COMPS,)),
            dma((COMPS,)),
        ],
        compiler_params=pltpu.CompilerParams(
            collective_id=0, has_side_effects=True, vmem_limit_bytes=60 << 20
        ),
        name="reduce_components",
    )(
        block_offsets.transpose(2, 1, 0),
        ports,
        surface,
        ports,
        surface,
        port_counts.reshape(1, CD),
        mode_shapes.reshape(CD * NBL, BS, M),
        block_values,
        conductance,
        capacity,
        coupling.reshape(CD * NP, BS, PB),
        boundary,
    )


def solution(mesh):
    in_specs = (
        P("comp", "port", None),
        P("comp", "port", None, None, None),
        P("comp", "port", None),
        P("comp", "port"),
        P("comp", "port"),
        P("comp", None, None, None),
        P("comp", None),
        P("comp", None),
        P("comp"),
        P(("comp", "port"), None, None),
    )
    out_specs = (P("comp", "port", None), P("comp", "port", None), P(("comp", "port"), None, None))
    return jax.shard_map(shards, mesh=mesh, in_specs=in_specs, out_specs=out_specs, check_vma=False)
```

```python
import jax
import jax.numpy as jnp
from jax import lax
from jax.experimental import pallas as pl
from jax.experimental.pallas import tpu as pltpu
from jax.sharding import PartitionSpec as P

BF, F32, I32 = jnp.bfloat16, jnp.float32, jnp.int32
COMPS, PORTS = 16, 8
CD, NBL, NB, NP = 16, 8, 3, 4
BS, M, PB = 128, 128, 256
HOPS = ((0, 1), (0, 3), (1, 0), (3, 0), (1, 1), (3, 3), (1, 3), (3, 1), (2, 0), (0, 2), (2, 3), (2, 1), (3, 2), (1, 2), (2, 2))
EARLY = 8
Z_HOPS = (4, 5, 2, 3, 6, 7, 1)
TOP = COMPS * 8


def nt(a, b):
    return lax.dot_general(a, b, (((1,), (1,)), ((), ())), preferred_element_type=F32)


def tn(a, b):
    return lax.dot_general(a, b, (((0,), (0,)), ((), ())), preferred_element_type=F32)


def remote(src, dst, send, recv, **where):
    return pltpu.make_async_remote_copy(
        src_ref=src,
        dst_ref=dst,
        send_sem=send,
        recv_sem=recv,
        device_id=where,
        device_id_type=pl.DeviceIdType.MESH,
    )


def fill_tables(me_port, ports_s, surface_s, ports_v, surface_v, counts_v, table):
    ports, surface = ports_v[...], surface_v[...]
    owner, target = (ports >> 1) & 7, ports >> 4
    shard = surface >> 3
    cell, device = shard * 8 + owner, ports >> 1
    comp = lax.broadcasted_iota(I32, (NP, CD), 1)
    slot = lax.broadcasted_iota(I32, (NP, CD), 0)
    order = comp * NP + slot
    alive = slot < counts_v[...]

    def count(c, ranks):
        in_cell, in_device = ranks
        for s in range(NP):
            port, block, at = ports_s[s, c], surface_s[s, c], c * NP + s
            this_device = port >> 1
            this_cell = (block >> 3) * 8 + (this_device & 7)
            later = order > at
            in_cell += jnp.where(later & (cell == this_cell), 1, 0)
            in_device += jnp.where(later & (device == this_device), 1, 0)
        return in_cell, in_device

    zero = jnp.zeros((NP, CD), I32)
    in_cell, in_device = lax.fori_loop(0, CD, count, (zero, zero))
    code = 2048 + (ports & 1) * 1024 + (shard * 2 + in_cell) * 64 + order
    here = alive & (owner == me_port)
    code = jnp.where(here, code, 0)
    device_key = target * 2 + in_device
    row = comp * NBL + (surface & 7)
    cell_key = jnp.where(shard == me_port, owner * 2 + in_cell, -1)
    q = lax.broadcasted_iota(I32, (TOP, CD), 0)
    wanted = (q >> 3) * 2 + (q & 1)
    total = jnp.zeros((TOP, CD), I32)
    for s in range(NP):
        total += jnp.where(device_key[s : s + 1] == wanted, code[s : s + 1], 0)
    table[0:TOP] = jnp.broadcast_to(jnp.sum(total, axis=1, keepdims=True), (TOP, 128))
    wanted = lax.broadcasted_iota(I32, (16, CD), 0)
    total = jnp.zeros((16, CD), I32)
    for s in range(NP):
        total += jnp.where(cell_key[s : s + 1] == wanted, row[s : s + 1], 0)
    table[TOP : TOP + 16] = jnp.broadcast_to(jnp.sum(total, axis=1, keepdims=True), (16, 128))


def kernel(
    offs,
    ports_s,
    surface_s,
    ports_v,
    surface_v,
    counts_v,
    shapes,
    values,
    cond_hbm,
    cap_hbm,
    coupling,
    boundary,
    sums_out,
    face_out,
    phi,
    vals,
    coup,
    cond,
    cap,
    bound,
    table,
    table_s,
    codes,
    codes_s,
    rows_out,
    rows_in,
    halo_lo,
    halo_hi,
    win,
    scaled,
    part,
    pair_in,
    zsum,
    z_in,
    fac_out,
    fac_in,
    late_out,
    late_in,
    both,
    acc,
    load_sem,
    vals_sem,
    rows_ss,
    rows_rs,
    halo_ss,
    halo_rs,
    pair_ss,
    pair_rs,
    z_ss,
    z_rs,
    fac_ss,
    fac_rs,
    code_ss,
    code_rs,
    late_ss,
    late_rs,
):
    c_me, p_me = lax.axis_index("comp"), lax.axis_index("port")
    y, x = c_me // 4, c_me % 4
    z, core = p_me // 2, p_me % 2
    before, after = (p_me + PORTS - 1) % PORTS, (p_me + 1) % PORTS

    def to_comp(hop):
        return ((y + hop[0]) % 4) * 4 + (x + hop[1]) % 4

    def from_comp(hop):
        return ((y + 4 - hop[0]) % 4) * 4 + (x + 4 - hop[1]) % 4

    barrier = pltpu.get_barrier_semaphore()

    @pl.loop(1, PORTS)
    def _(j):
        pl.semaphore_signal(barrier, 1, device_id={"port": (p_me + j) % PORTS}, device_id_type=pl.DeviceIdType.MESH)

    for hop in HOPS:
        pl.semaphore_signal(barrier, 1, device_id={"comp": to_comp(hop)}, device_id_type=pl.DeviceIdType.MESH)

    load_phi = pltpu.make_async_copy(shapes, phi, load_sem.at[0])
    load_coup = pltpu.make_async_copy(coupling, coup, load_sem.at[1])
    load_cond = pltpu.make_async_copy(cond_hbm, cond, load_sem.at[2])
    load_cap = pltpu.make_async_copy(cap_hbm, cap, load_sem.at[3])
    load_bound = pltpu.make_async_copy(boundary, bound, load_sem.at[4])
    load_phi.start()
    load_coup.start()
    load_cond.start()
    load_cap.start()

    def load_vals(c):
        return pltpu.make_async_copy(values.at[c], vals.at[c], vals_sem.at[c])

    @pl.loop(0, CD)
    def _(c):
        load_vals(c).start()

    load_bound.start()
    fill_tables(p_me, ports_s, surface_s, ports_v, surface_v, counts_v, table)
    to_smem = pltpu.make_async_copy(table, table_s, load_sem.at[5])
    to_smem.start()
    load_phi.wait()
    to_smem.wait()

    @pl.loop(0, PORTS)
    def _(o):
        for k in range(2):
            picked = table_s[TOP + 2 * o + k, 0]
            rows_out[o, k] = phi[picked].T

    rows_in[p_me] = rows_out[p_me]
    codes[pl.ds(pl.multiple_of(c_me * 8, 8), 8)] = table[pl.ds(pl.multiple_of(c_me * 8, 8), 8)]
    pl.semaphore_wait(barrier, PORTS - 1 + COMPS - 1)

    def send_rows(j):
        o = (p_me + j) % PORTS
        return remote(rows_out.at[o], rows_in.at[p_me], rows_ss.at[o], rows_rs.at[p_me], port=o)

    def recv_rows(j):
        o = (p_me + PORTS - j) % PORTS
        return remote(rows_out.at[o], rows_in.at[o], rows_ss.at[o], rows_rs.at[o], port=o)

    for j in Z_HOPS:
        send_rows(j).start()

    def send_up(c):
        return remote(
            shapes.at[pl.ds(c * NBL + NBL - 2, 2)], halo_lo.at[c], halo_ss.at[0, c], halo_rs.at[0, c], port=after
        )

    def send_down(c):
        return remote(shapes.at[pl.ds(c * NBL, 2)], halo_hi.at[c], halo_ss.at[1, c], halo_rs.at[1, c], port=before)

    @pl.loop(0, CD)
    def _(c):
        send_up(c).start()
        send_down(c).start()

    def send_codes(hop):
        d = to_comp(hop)
        return remote(
            table.at[pl.ds(pl.multiple_of(d * 8, 8), 8)],
            codes.at[pl.ds(pl.multiple_of(c_me * 8, 8), 8)],
            code_ss.at[d],
            code_rs.at[c_me],
            comp=d,
        )

    def recv_codes(hop):
        d = from_comp(hop)
        return remote(
            table.at[pl.ds(pl.multiple_of(d * 8, 8), 8)],
            codes.at[pl.ds(pl.multiple_of(d * 8, 8), 8)],
            code_ss.at[d],
            code_rs.at[d],
            comp=d,
        )

    def send_factors(hop):
        d = to_comp(hop)
        return remote(fac_out.at[d], fac_in.at[c_me], fac_ss.at[d], fac_rs.at[c_me], comp=d)

    def recv_factors(hop):
        d = from_comp(hop)
        return remote(fac_out.at[d], fac_in.at[d], fac_ss.at[d], fac_rs.at[d], comp=d)

    def send_late(hop):
        d = to_comp(hop)
        return remote(late_out.at[d], late_in.at[c_me], late_ss.at[d], late_rs.at[c_me], comp=d)

    def recv_late(hop):
        d = from_comp(hop)
        return remote(late_out.at[d], late_in.at[d], late_ss.at[d], late_rs.at[d], comp=d)

    load_coup.wait()
    for hop in HOPS[:EARLY]:
        d = to_comp(hop)
        for k in range(2):
            fac_out[d, pl.ds(k * M, M)] = coup[table_s[d * 8 + k, 0] & 63]
        send_factors(hop).start()

    for hop in HOPS:
        send_codes(hop).start()

    @pl.loop(1, PORTS)
    def _(j):
        recv_rows(j).wait_recv()

    def row_of(code):
        return rows_in[(code >> 7) & 7, (code >> 6) & 1]

    def factor(d, k):
        code = table_s[d * 8 + k, 0]
        return jnp.dot(row_of(code), coup[code & 63], preferred_element_type=F32).astype(BF)

    for hop in HOPS[:EARLY]:
        d = to_comp(hop)
        for k in range(2):
            late_out[d, k] = row_of(table_s[d * 8 + k, 0])
        send_late(hop).start()
    for hop in HOPS[EARLY:]:
        d = to_comp(hop)
        for k in range(2):
            fac_out[d, pl.ds(k * M, M)] = factor(d, k)
        send_factors(hop).start()

    for k in range(2):
        fac_in[c_me, pl.ds(k * M, M)] = factor(c_me, k)

    def send_pair(c):
        return remote(
            part.at[1 - core, :, c], pair_in.at[:, c], pair_ss.at[c], pair_rs.at[c], port=2 * z + 1 - core
        )

    def send_z(d, h):
        to = (z + d) % 4
        return remote(
            zsum.at[to, pl.ds(2 * h, 2)], z_in.at[z, pl.ds(2 * h, 2)], z_ss.at[to, h], z_rs.at[z, h], port=2 * to + core
        )

    def recv_z(d, h):
        at = (z + 4 - d) % 4
        return remote(
            zsum.at[at, pl.ds(2 * h, 2)], z_in.at[at, pl.ds(2 * h, 2)], z_ss.at[at, h], z_rs.at[at, h], port=2 * at + core
        )

    def chip_sums(h):
        for i in range(2):
            c = 2 * h + i
            send_pair(c).wait_recv()
            zsum[:, c] = part[core, :, c] + pair_in[:, c]
        for d in range(1, 4):
            send_z(d, h).start()

    first = jnp.where(p_me == 0, 0.0, 1.0)
    last = jnp.where(p_me == PORTS - 1, 0.0, 1.0)

    def modal(c):
        load_vals(c).wait()
        send_up(c).wait_recv()
        send_down(c).wait_recv()
        for i in range(2):
            win[i] = (halo_lo[c, i].astype(F32) * first).T.astype(BF)
            win[NBL + 2 + i] = (halo_hi[c, i].astype(F32) * last).T.astype(BF)
        for r in range(NBL):
            win[2 + r] = phi[c * NBL + r].T
        base = pl.multiple_of((c // 8) * 8, 8)
        mine = lax.broadcasted_iota(I32, (8, NBL * BS), 0) == c % 8
        cond_row = jnp.sum(jnp.where(mine, cond[pl.ds(base, 8)], 0.0), axis=0, keepdims=True)
        cap_row = jnp.sum(jnp.where(mine, cap[pl.ds(base, 8)], 0.0), axis=0, keepdims=True)
        for r in range(NBL):
            cells = slice(r * BS, (r + 1) * BS)
            near = jnp.concatenate([win[r + 2 + offs[k, r, c]] for k in range(NB)], axis=1)
            blocks = jnp.concatenate([vals[c, r, k] for k in range(NB)], axis=1)
            own = win[r + 2].astype(F32)
            scaled[0:M, cells] = (nt(near, blocks) + cond_row[:, cells] * own).astype(BF)
            scaled[M : 2 * M, cells] = (cap_row[:, cells] * own).astype(BF)
        every = jnp.concatenate([win[r + 2] for r in range(NBL)], axis=1)
        sums = nt(every, scaled[...])
        for p in range(PORTS):
            part[p % 2, p // 2, c] = sums[16 * p : 16 * p + 16]

    load_cond.wait()
    load_cap.wait()

    @pl.loop(0, CD // 2)
    def _(h):
        @pl.loop(0, 2)
        def _(i):
            modal(2 * h + i)
            send_pair(2 * h + i).start()

        @pl.when(h > 0)
        def _():
            chip_sums(h - 1)

    chip_sums(CD // 2 - 1)

    for hop in HOPS:
        recv_codes(hop).wait_recv()
    to_smem = pltpu.make_async_copy(codes, codes_s, load_sem.at[6])
    to_smem.start()
    acc[...] = jnp.zeros_like(acc)
    to_smem.wait()

    def square(d, factors):
        for o in range(2):
            halves = []
            for k in range(2):
                code = codes_s[d * 8 + k, 0]
                weight = jnp.where((code >> 10) == 2 + o, 1.0, 0.0).astype(F32)
                halves.append((factors[pl.ds(k * M, M)].astype(F32) * weight).astype(BF))
            acc[o] += tn(jnp.concatenate(halves, axis=0), factors[...])

    square(c_me, fac_in.at[c_me])
    for hop in HOPS[:EARLY]:
        d = from_comp(hop)
        recv_factors(hop).wait_recv()
        recv_late(hop).wait_recv()
        for k in range(2):
            half = pl.ds(k * M, M)
            both[half] = jnp.dot(late_in[d, k], fac_in[d, half], preferred_element_type=F32).astype(BF)
        square(d, both)
    for hop in HOPS[EARLY:]:
        recv_factors(hop).wait_recv()
        square(from_comp(hop), fac_in.at[from_comp(hop)])

    load_bound.wait()
    face_out[...] = bound[...] + acc[...] * (1.0 / M)

    @pl.loop(0, CD // 2)
    def _(h):
        for d in range(1, 4):
            recv_z(d, h).wait_recv()
        for i in range(2):
            c = 2 * h + i
            total = zsum[z, c]
            for d in range(1, 4):
                total = total + z_in[(z + 4 - d) % 4, c]
            sums_out[c] = total
        for d in range(1, 4):
            send_z(d, h).wait_send()

    @pl.loop(0, CD)
    def _(c):
        send_up(c).wait_send()
        send_down(c).wait_send()
        send_pair(c).wait_send()

    @pl.loop(1, PORTS)
    def _(j):
        send_rows(j).wait_send()

    for hop in HOPS:
        send_factors(hop).wait_send()
        send_codes(hop).wait_send()
    for hop in HOPS[:EARLY]:
        send_late(hop).wait_send()


def finish(sums, face, cond_out, cap_out, face_out):
    cond_out[...] = sums[:, :, 0:M]
    cap_out[...] = sums[:, :, M : 2 * M]
    face_out[...] = face[...]


def shards(
    mode_shapes,
    block_values,
    block_offsets,
    conductance,
    capacity,
    coupling,
    surface_blocks,
    port_ids,
    port_counts,
    boundary,
):
    smem = pl.BlockSpec(memory_space=pltpu.SMEM)
    vmem = pl.BlockSpec(memory_space=pltpu.VMEM)
    hbm = pl.BlockSpec(memory_space=pltpu.HBM)
    dma = pltpu.SemaphoreType.DMA
    ports, surface = port_ids.T, surface_blocks.T
    modal = jax.ShapeDtypeStruct((CD, M // PORTS, M), F32)
    sums, face = pl.pallas_call(
        kernel,
        out_shape=(
            jax.ShapeDtypeStruct((CD, M // PORTS, 2 * M), F32),
            jax.ShapeDtypeStruct((2, PB, PB), F32),
        ),
        in_specs=[smem] * 3 + [vmem] * 3 + [hbm] * 6,
        out_specs=(vmem, vmem),
        scratch_shapes=[
            pltpu.VMEM((CD * NBL, BS, M), BF),
            pltpu.VMEM((CD, NBL, NB, BS, BS), BF),
            pltpu.VMEM((CD * NP, BS, PB), BF),
            pltpu.VMEM((CD, NBL * BS), F32),
            pltpu.VMEM((CD, NBL * BS), F32),
            pltpu.VMEM((2, PB, PB), F32),
            pltpu.VMEM((TOP + 16, 128), I32),
            pltpu.SMEM((TOP + 16, 128), I32),
            pltpu.VMEM((TOP, 128), I32),
            pltpu.SMEM((TOP, 128), I32),
            pltpu.VMEM((PORTS, 2, M, BS), BF),
            pltpu.VMEM((PORTS, 2, M, BS), BF),
            pltpu.VMEM((CD, 2, BS, M), BF),
            pltpu.VMEM((CD, 2, BS, M), BF),
            pltpu.VMEM((NBL + 4, M, BS), BF),
            pltpu.VMEM((2 * M, NBL * BS), BF),
            pltpu.VMEM((2, 4, CD, 16, 2 * M), F32),
            pltpu.VMEM((4, CD, 16, 2 * M), F32),
            pltpu.VMEM((4, CD, 16, 2 * M), F32),
            pltpu.VMEM((4, CD, 16, 2 * M), F32),
            pltpu.VMEM((COMPS, 2 * M, PB), BF),
            pltpu.VMEM((COMPS, 2 * M, PB), BF),
            pltpu.VMEM((COMPS, 2, M, BS), BF),
            pltpu.VMEM((COMPS, 2, M, BS), BF),
            pltpu.VMEM((2 * M, PB), BF),
            pltpu.VMEM((2, PB, PB), F32),
            dma((7,)),
            dma((CD,)),
            dma((PORTS,)),
            dma((PORTS,)),
            dma((2, CD)),
            dma((2, CD)),
            dma((CD,)),
            dma((CD,)),
            dma((4, CD // 2)),
            dma((4, CD // 2)),
            dma((COMPS,)),
            dma((COMPS,)),
            dma((COMPS,)),
            dma((COMPS,)),
            dma((COMPS,)),
            dma((COMPS,)),
        ],
        compiler_params=pltpu.CompilerParams(
            collective_id=0, has_side_effects=True, vmem_limit_bytes=63 << 20
        ),
        name="reduce_components",
    )(
        block_offsets.transpose(2, 1, 0),
        ports,
        surface,
        ports,
        surface,
        port_counts.reshape(1, CD),
        mode_shapes.reshape(CD * NBL, BS, M),
        block_values,
        conductance,
        capacity,
        coupling.reshape(CD * NP, BS, PB),
        boundary,
    )
    return pl.pallas_call(
        finish,
        out_shape=(modal, modal, jax.ShapeDtypeStruct((2, PB, PB), F32)),
        in_specs=[vmem, vmem],
        out_specs=(vmem, vmem, vmem),
        compiler_params=pltpu.CompilerParams(vmem_limit_bytes=63 << 20),
        name="finish",
    )(sums, face)


def solution(mesh):
    in_specs = (
        P("comp", "port", None),
        P("comp", "port", None, None, None),
        P("comp", "port", None),
        P("comp", "port"),
        P("comp", "port"),
        P("comp", None, None, None),
        P("comp", None),
        P("comp", None),
        P("comp"),
        P(("comp", "port"), None, None),
    )
    out_specs = (P("comp", "port", None), P("comp", "port", None), P(("comp", "port"), None, None))
    return jax.shard_map(shards, mesh=mesh, in_specs=in_specs, out_specs=out_specs, check_vma=False)
```

```python
import jax
import jax.numpy as jnp
from jax import lax
from jax.experimental import pallas as pl
from jax.experimental.pallas import tpu as pltpu
from jax.sharding import PartitionSpec as P

BF, F32, I32 = jnp.bfloat16, jnp.float32, jnp.int32
COMPS, PORTS = 16, 8
CD, NBL, NB, NP = 16, 8, 3, 4
BS, M, PB = 128, 128, 256
HOPS = ((0, 1), (0, 3), (1, 0), (3, 0), (1, 1), (3, 3), (1, 3), (3, 1), (2, 0), (0, 2), (2, 3), (2, 1), (3, 2), (1, 2), (2, 2))
EARLY = 8
LAST = 3
AHEAD = 12
Z_HOPS = (4, 5, 2, 3, 6, 7, 1)
TOP = COMPS * 8


def nt(a, b):
    return lax.dot_general(a, b, (((1,), (1,)), ((), ())), preferred_element_type=F32)


def tn(a, b):
    return lax.dot_general(a, b, (((0,), (0,)), ((), ())), preferred_element_type=F32)


def remote(src, dst, send, recv, **where):
    return pltpu.make_async_remote_copy(
        src_ref=src,
        dst_ref=dst,
        send_sem=send,
        recv_sem=recv,
        device_id=where,
        device_id_type=pl.DeviceIdType.MESH,
    )


def fill_tables(me_port, ports_s, surface_s, ports_v, surface_v, counts_v, table):
    ports, surface = ports_v[...], surface_v[...]
    owner, target = (ports >> 1) & 7, ports >> 4
    shard = surface >> 3
    cell, device = shard * 8 + owner, ports >> 1
    comp = lax.broadcasted_iota(I32, (NP, CD), 1)
    slot = lax.broadcasted_iota(I32, (NP, CD), 0)
    order = comp * NP + slot
    alive = slot < counts_v[...]

    def count(c, ranks):
        in_cell, in_device = ranks
        for s in range(NP):
            port, block, at = ports_s[s, c], surface_s[s, c], c * NP + s
            this_device = port >> 1
            this_cell = (block >> 3) * 8 + (this_device & 7)
            later = order > at
            in_cell += jnp.where(later & (cell == this_cell), 1, 0)
            in_device += jnp.where(later & (device == this_device), 1, 0)
        return in_cell, in_device

    zero = jnp.zeros((NP, CD), I32)
    in_cell, in_device = lax.fori_loop(0, CD, count, (zero, zero))
    code = 2048 + (ports & 1) * 1024 + (shard * 2 + in_cell) * 64 + order
    here = alive & (owner == me_port)
    code = jnp.where(here, code, 0)
    device_key = target * 2 + in_device
    row = comp * NBL + (surface & 7)
    cell_key = jnp.where(shard == me_port, owner * 2 + in_cell, -1)
    q = lax.broadcasted_iota(I32, (TOP, CD), 0)
    wanted = (q >> 3) * 2 + (q & 1)
    total = jnp.zeros((TOP, CD), I32)
    for s in range(NP):
        total += jnp.where(device_key[s : s + 1] == wanted, code[s : s + 1], 0)
    table[0:TOP] = jnp.broadcast_to(jnp.sum(total, axis=1, keepdims=True), (TOP, 128))
    wanted = lax.broadcasted_iota(I32, (16, CD), 0)
    total = jnp.zeros((16, CD), I32)
    for s in range(NP):
        total += jnp.where(cell_key[s : s + 1] == wanted, row[s : s + 1], 0)
    table[TOP : TOP + 16] = jnp.broadcast_to(jnp.sum(total, axis=1, keepdims=True), (16, 128))


def kernel(
    offs,
    ports_s,
    surface_s,
    ports_v,
    surface_v,
    counts_v,
    shapes,
    values,
    cond_hbm,
    cap_hbm,
    coupling,
    boundary,
    sums_out,
    face_out,
    phi,
    phi_t,
    vals,
    coup,
    cond,
    cap,
    bound,
    table,
    table_s,
    codes,
    codes_s,
    rows_out,
    rows_in,
    halo_lo,
    halo_hi,
    win,
    scaled,
    part,
    pair_in,
    zsum,
    z_in,
    fac_out,
    fac_in,
    late_out,
    late_in,
    both,
    acc,
    load_sem,
    vals_sem,
    rows_ss,
    rows_rs,
    halo_ss,
    halo_rs,
    pair_ss,
    pair_rs,
    z_ss,
    z_rs,
    fac_ss,
    fac_rs,
    code_ss,
    code_rs,
    late_ss,
    late_rs,
):
    c_me, p_me = lax.axis_index("comp"), lax.axis_index("port")
    y, x = c_me // 4, c_me % 4
    z, core = p_me // 2, p_me % 2
    before, after = (p_me + PORTS - 1) % PORTS, (p_me + 1) % PORTS

    def to_comp(hop):
        return ((y + hop[0]) % 4) * 4 + (x + hop[1]) % 4

    def from_comp(hop):
        return ((y + 4 - hop[0]) % 4) * 4 + (x + 4 - hop[1]) % 4

    barrier = pltpu.get_barrier_semaphore()

    @pl.loop(1, PORTS)
    def _(j):
        pl.semaphore_signal(barrier, 1, device_id={"port": (p_me + j) % PORTS}, device_id_type=pl.DeviceIdType.MESH)

    for hop in HOPS:
        pl.semaphore_signal(barrier, 1, device_id={"comp": to_comp(hop)}, device_id_type=pl.DeviceIdType.MESH)

    load_phi = pltpu.make_async_copy(shapes, phi, load_sem.at[0])
    load_coup = pltpu.make_async_copy(coupling, coup, load_sem.at[1])
    load_cond = pltpu.make_async_copy(cond_hbm, cond, load_sem.at[2])
    load_cap = pltpu.make_async_copy(cap_hbm, cap, load_sem.at[3])
    load_bound = pltpu.make_async_copy(boundary, bound, load_sem.at[4])
    load_phi.start()
    load_coup.start()
    load_cond.start()
    load_cap.start()

    def load_vals(c):
        return pltpu.make_async_copy(values.at[c], vals.at[c], vals_sem.at[c])

    @pl.loop(0, CD)
    def _(c):
        load_vals(c).start()

    load_bound.start()
    fill_tables(p_me, ports_s, surface_s, ports_v, surface_v, counts_v, table)
    to_smem = pltpu.make_async_copy(table, table_s, load_sem.at[5])
    to_smem.start()
    load_phi.wait()
    to_smem.wait()

    @pl.loop(0, PORTS)
    def _(o):
        for k in range(2):
            picked = table_s[TOP + 2 * o + k, 0]
            rows_out[o, k] = phi[picked].T

    load_coup.wait()
    for hop in HOPS[:EARLY]:
        d = to_comp(hop)
        for k in range(2):
            fac_out[d, pl.ds(k * M, M)] = coup[table_s[d * 8 + k, 0] & 63]

    rows_in[p_me] = rows_out[p_me]
    codes[pl.ds(pl.multiple_of(c_me * 8, 8), 8)] = table[pl.ds(pl.multiple_of(c_me * 8, 8), 8)]
    pl.semaphore_wait(barrier, PORTS - 1 + COMPS - 1)

    def send_rows(j):
        o = (p_me + j) % PORTS
        return remote(rows_out.at[o], rows_in.at[p_me], rows_ss.at[o], rows_rs.at[p_me], port=o)

    def recv_rows(j):
        o = (p_me + PORTS - j) % PORTS
        return remote(rows_out.at[o], rows_in.at[o], rows_ss.at[o], rows_rs.at[o], port=o)

    for j in Z_HOPS:
        send_rows(j).start()

    def send_codes(hop):
        d = to_comp(hop)
        return remote(
            table.at[pl.ds(pl.multiple_of(d * 8, 8), 8)],
            codes.at[pl.ds(pl.multiple_of(c_me * 8, 8), 8)],
            code_ss.at[d],
            code_rs.at[c_me],
            comp=d,
        )

    def recv_codes(hop):
        d = from_comp(hop)
        return remote(
            table.at[pl.ds(pl.multiple_of(d * 8, 8), 8)],
            codes.at[pl.ds(pl.multiple_of(d * 8, 8), 8)],
            code_ss.at[d],
            code_rs.at[d],
            comp=d,
        )

    def send_factors(hop):
        d = to_comp(hop)
        return remote(fac_out.at[d], fac_in.at[c_me], fac_ss.at[d], fac_rs.at[c_me], comp=d)

    def recv_factors(hop):
        d = from_comp(hop)
        return remote(fac_out.at[d], fac_in.at[d], fac_ss.at[d], fac_rs.at[d], comp=d)

    def send_late(hop):
        d = to_comp(hop)
        return remote(late_out.at[d], late_in.at[c_me], late_ss.at[d], late_rs.at[c_me], comp=d)

    def recv_late(hop):
        d = from_comp(hop)
        return remote(late_out.at[d], late_in.at[d], late_ss.at[d], late_rs.at[d], comp=d)

    for hop in HOPS[:EARLY]:
        send_factors(hop).start()
    for hop in HOPS:
        send_codes(hop).start()

    def send_up(c):
        return remote(
            shapes.at[pl.ds(c * NBL + NBL - 2, 2)], halo_lo.at[c], halo_ss.at[0, c], halo_rs.at[0, c], port=after
        )

    def send_down(c):
        return remote(shapes.at[pl.ds(c * NBL, 2)], halo_hi.at[c], halo_ss.at[1, c], halo_rs.at[1, c], port=before)

    @pl.loop(0, CD)
    def _(c):
        send_up(c).start()
        send_down(c).start()

    def inner(c):
        load_vals(c).wait()
        for r in range(NBL):
            phi_t[c * NBL + r] = phi[c * NBL + r].T
        cond_row, cap_row = row_of_cells(cond, c), row_of_cells(cap, c)
        for r in range(NBL):
            cells = slice(r * BS, (r + 1) * BS)
            own = phi_t[c * NBL + r].astype(F32)
            scaled[c, M : 2 * M, cells] = (cap_row[:, cells] * own).astype(BF)
            if 2 <= r < NBL - 2:
                near = jnp.concatenate([phi_t[c * NBL + r + offs[k, r, c]] for k in range(NB)], axis=1)
                scaled[c, 0:M, cells] = block_row(c, r, near, own, cond_row)

    def row_of_cells(source, c):
        mine = lax.broadcasted_iota(I32, (8, NBL * BS), 0) == c % 8
        return jnp.sum(jnp.where(mine, source[pl.ds(pl.multiple_of((c // 8) * 8, 8), 8)], 0.0), axis=0, keepdims=True)

    def block_row(c, r, near, own, cond_row):
        blocks = jnp.concatenate([vals[c, r, k] for k in range(NB)], axis=1)
        return (nt(near, blocks) + cond_row[:, r * BS : (r + 1) * BS] * own).astype(BF)

    load_cond.wait()
    load_cap.wait()
    pl.loop(0, AHEAD)(inner)

    @pl.loop(1, PORTS)
    def _(j):
        recv_rows(j).wait_recv()

    def row_of(code):
        return rows_in[(code >> 7) & 7, (code >> 6) & 1]

    def factor(d, k):
        code = table_s[d * 8 + k, 0]
        return jnp.dot(row_of(code), coup[code & 63], preferred_element_type=F32).astype(BF)

    for hop in HOPS[:EARLY]:
        d = to_comp(hop)
        for k in range(2):
            late_out[d, k] = row_of(table_s[d * 8 + k, 0])
        send_late(hop).start()
    for hop in HOPS[EARLY:]:
        d = to_comp(hop)
        for k in range(2):
            fac_out[d, pl.ds(k * M, M)] = factor(d, k)
        send_factors(hop).start()

    for k in range(2):
        fac_in[c_me, pl.ds(k * M, M)] = factor(c_me, k)

    def send_pair(c):
        return remote(
            part.at[1 - core, :, c], pair_in.at[:, c], pair_ss.at[c], pair_rs.at[c], port=2 * z + 1 - core
        )

    def send_z(d, h):
        to = (z + d) % 4
        return remote(
            zsum.at[to, pl.ds(2 * h, 2)], z_in.at[z, pl.ds(2 * h, 2)], z_ss.at[to, h], z_rs.at[z, h], port=2 * to + core
        )

    def recv_z(d, h):
        at = (z + 4 - d) % 4
        return remote(
            zsum.at[at, pl.ds(2 * h, 2)], z_in.at[at, pl.ds(2 * h, 2)], z_ss.at[at, h], z_rs.at[at, h], port=2 * at + core
        )

    def chip_sums(h):
        for i in range(2):
            c = 2 * h + i
            send_pair(c).wait_recv()
            zsum[:, c] = part[core, :, c] + pair_in[:, c]
        for d in range(1, 4):
            send_z(d, h).start()

    first = jnp.where(p_me == 0, 0.0, 1.0)
    last = jnp.where(p_me == PORTS - 1, 0.0, 1.0)

    def modal(c):
        send_up(c).wait_recv()
        send_down(c).wait_recv()
        for i in range(2):
            win[i] = (halo_lo[c, i].astype(F32) * first).T.astype(BF)
            win[NBL + 2 + i] = (halo_hi[c, i].astype(F32) * last).T.astype(BF)
        for r in range(NBL):
            win[2 + r] = phi_t[c * NBL + r]
        cond_row = row_of_cells(cond, c)
        for r in (0, 1, NBL - 2, NBL - 1):
            near = jnp.concatenate([win[r + 2 + offs[k, r, c]] for k in range(NB)], axis=1)
            scaled[c, 0:M, r * BS : (r + 1) * BS] = block_row(c, r, near, win[r + 2].astype(F32), cond_row)
        every = jnp.concatenate([phi_t[c * NBL + r] for r in range(NBL)], axis=1)
        sums = nt(every, scaled[c])
        for p in range(PORTS):
            part[p % 2, p // 2, c] = sums[16 * p : 16 * p + 16]

    pl.loop(AHEAD, CD)(inner)

    @pl.loop(0, CD // 2)
    def _(h):
        @pl.loop(0, 2)
        def _(i):
            modal(2 * h + i)
            send_pair(2 * h + i).start()

        @pl.when(h > 0)
        def _():
            chip_sums(h - 1)

    chip_sums(CD // 2 - 1)

    def gather_sums():
        @pl.loop(0, CD // 2)
        def _(h):
            for d in range(1, 4):
                recv_z(d, h).wait_recv()
            for i in range(2):
                c = 2 * h + i
                total = zsum[z, c]
                for d in range(1, 4):
                    total = total + z_in[(z + 4 - d) % 4, c]
                sums_out[c] = total
            for d in range(1, 4):
                send_z(d, h).wait_send()

    for hop in HOPS:
        recv_codes(hop).wait_recv()
    to_smem = pltpu.make_async_copy(codes, codes_s, load_sem.at[6])
    to_smem.start()
    acc[...] = jnp.zeros_like(acc)
    to_smem.wait()

    def square(d, factors):
        for o in range(2):
            halves = []
            for k in range(2):
                code = codes_s[d * 8 + k, 0]
                weight = jnp.where((code >> 10) == 2 + o, 1.0, 0.0).astype(F32)
                halves.append((factors[pl.ds(k * M, M)].astype(F32) * weight).astype(BF))
            acc[o] += tn(jnp.concatenate(halves, axis=0), factors[...])

    square(c_me, fac_in.at[c_me])
    for hop in HOPS[:EARLY]:
        d = from_comp(hop)
        recv_factors(hop).wait_recv()
        recv_late(hop).wait_recv()
        for k in range(2):
            half = pl.ds(k * M, M)
            both[half] = jnp.dot(late_in[d, k], fac_in[d, half], preferred_element_type=F32).astype(BF)
        square(d, both)
    for at, hop in enumerate(HOPS[EARLY:]):
        if at == len(HOPS) - EARLY - LAST:
            gather_sums()
        recv_factors(hop).wait_recv()
        square(from_comp(hop), fac_in.at[from_comp(hop)])

    load_bound.wait()
    face_out[...] = bound[...] + acc[...] * (1.0 / M)

    @pl.loop(0, CD)
    def _(c):
        send_up(c).wait_send()
        send_down(c).wait_send()
        send_pair(c).wait_send()

    @pl.loop(1, PORTS)
    def _(j):
        send_rows(j).wait_send()

    for hop in HOPS:
        send_factors(hop).wait_send()
        send_codes(hop).wait_send()
    for hop in HOPS[:EARLY]:
        send_late(hop).wait_send()


def finish(sums, face, cond_out, cap_out, face_out):
    cond_out[...] = sums[:, :, 0:M]
    cap_out[...] = sums[:, :, M : 2 * M]
    face_out[...] = face[...]


def shards(
    mode_shapes,
    block_values,
    block_offsets,
    conductance,
    capacity,
    coupling,
    surface_blocks,
    port_ids,
    port_counts,
    boundary,
):
    smem = pl.BlockSpec(memory_space=pltpu.SMEM)
    vmem = pl.BlockSpec(memory_space=pltpu.VMEM)
    hbm = pl.BlockSpec(memory_space=pltpu.HBM)
    dma = pltpu.SemaphoreType.DMA
    ports, surface = port_ids.T, surface_blocks.T
    modal = jax.ShapeDtypeStruct((CD, M // PORTS, M), F32)
    sums, face = pl.pallas_call(
        kernel,
        out_shape=(
            pltpu.VMEM((CD, M // PORTS, 2 * M), F32),
            pltpu.VMEM((2, PB, PB), F32),
        ),
        in_specs=[smem] * 3 + [vmem] * 3 + [hbm] * 6,
        out_specs=(vmem, vmem),
        scratch_shapes=[
            pltpu.VMEM((CD * NBL, BS, M), BF),
            pltpu.VMEM((CD * NBL, M, BS), BF),
            pltpu.VMEM((CD, NBL, NB, BS, BS), BF),
            pltpu.VMEM((CD * NP, BS, PB), BF),
            pltpu.VMEM((CD, NBL * BS), F32),
            pltpu.VMEM((CD, NBL * BS), F32),
            pltpu.VMEM((2, PB, PB), F32),
            pltpu.VMEM((TOP + 16, 128), I32),
            pltpu.SMEM((TOP + 16, 128), I32),
            pltpu.VMEM((TOP, 128), I32),
            pltpu.SMEM((TOP, 128), I32),
            pltpu.VMEM((PORTS, 2, M, BS), BF),
            pltpu.VMEM((PORTS, 2, M, BS), BF),
            pltpu.VMEM((CD, 2, BS, M), BF),
            pltpu.VMEM((CD, 2, BS, M), BF),
            pltpu.VMEM((NBL + 4, M, BS), BF),
            pltpu.VMEM((CD, 2 * M, NBL * BS), BF),
            pltpu.VMEM((2, 4, CD, 16, 2 * M), F32),
            pltpu.VMEM((4, CD, 16, 2 * M), F32),
            pltpu.VMEM((4, CD, 16, 2 * M), F32),
            pltpu.VMEM((4, CD, 16, 2 * M), F32),
            pltpu.VMEM((COMPS, 2 * M, PB), BF),
            pltpu.VMEM((COMPS, 2 * M, PB), BF),
            pltpu.VMEM((COMPS, 2, M, BS), BF),
            pltpu.VMEM((COMPS, 2, M, BS), BF),
            pltpu.VMEM((2 * M, PB), BF),
            pltpu.VMEM((2, PB, PB), F32),
            dma((7,)),
            dma((CD,)),
            dma((PORTS,)),
            dma((PORTS,)),
            dma((2, CD)),
            dma((2, CD)),
            dma((CD,)),
            dma((CD,)),
            dma((4, CD // 2)),
            dma((4, CD // 2)),
            dma((COMPS,)),
            dma((COMPS,)),
            dma((COMPS,)),
            dma((COMPS,)),
            dma((COMPS,)),
            dma((COMPS,)),
        ],
        compiler_params=pltpu.CompilerParams(
            collective_id=0, has_side_effects=True, vmem_limit_bytes=62 << 20
        ),
        name="reduce_components",
    )(
        block_offsets.transpose(2, 1, 0),
        ports,
        surface,
        ports,
        surface,
        port_counts.reshape(1, CD),
        mode_shapes.reshape(CD * NBL, BS, M),
        block_values,
        conductance,
        capacity,
        coupling.reshape(CD * NP, BS, PB),
        boundary,
    )
    return pl.pallas_call(
        finish,
        out_shape=(modal, modal, jax.ShapeDtypeStruct((2, PB, PB), F32)),
        in_specs=[vmem, vmem],
        out_specs=(vmem, vmem, vmem),
        compiler_params=pltpu.CompilerParams(vmem_limit_bytes=62 << 20),
        name="finish",
    )(pltpu.with_memory_space_constraint(sums, pltpu.VMEM), pltpu.with_memory_space_constraint(face, pltpu.VMEM))


def solution(mesh):
    in_specs = (
        P("comp", "port", None),
        P("comp", "port", None, None, None),
        P("comp", "port", None),
        P("comp", "port"),
        P("comp", "port"),
        P("comp", None, None, None),
        P("comp", None),
        P("comp", None),
        P("comp"),
        P(("comp", "port"), None, None),
    )
    out_specs = (P("comp", "port", None), P("comp", "port", None), P(("comp", "port"), None, None))
    return jax.shard_map(shards, mesh=mesh, in_specs=in_specs, out_specs=out_specs, check_vma=False)
```

```python
import jax
import jax.numpy as jnp
from jax import lax
from jax.experimental import pallas as pl
from jax.experimental.pallas import tpu as pltpu
from jax.sharding import PartitionSpec as P

BF, F32, I32 = jnp.bfloat16, jnp.float32, jnp.int32
COMPS, PORTS = 16, 8
CD, NBL, NB, NP = 16, 8, 3, 4
BS, M, PB = 128, 128, 256
HOPS = ((0, 1), (0, 3), (1, 0), (3, 0), (1, 1), (3, 3), (1, 3), (3, 1), (2, 0), (0, 2), (2, 3), (2, 1), (3, 2), (1, 2), (2, 2))
EARLY = 10
LAST = 3
AHEAD = 12
Z_HOPS = (4, 5, 2, 3, 6, 7, 1)
TOP = COMPS * 8


def nt(a, b):
    return lax.dot_general(a, b, (((1,), (1,)), ((), ())), preferred_element_type=F32)


def tn(a, b):
    return lax.dot_general(a, b, (((0,), (0,)), ((), ())), preferred_element_type=F32)


def remote(src, dst, send, recv, **where):
    return pltpu.make_async_remote_copy(
        src_ref=src,
        dst_ref=dst,
        send_sem=send,
        recv_sem=recv,
        device_id=where,
        device_id_type=pl.DeviceIdType.MESH,
    )


def fill_tables(me_port, ports_s, surface_s, ports_v, surface_v, counts_v, table):
    ports, surface = ports_v[...], surface_v[...]
    owner, target = (ports >> 1) & 7, ports >> 4
    shard = surface >> 3
    cell, device = shard * 8 + owner, ports >> 1
    comp = lax.broadcasted_iota(I32, (NP, CD), 1)
    slot = lax.broadcasted_iota(I32, (NP, CD), 0)
    order = comp * NP + slot
    alive = slot < counts_v[...]

    def count(c, ranks):
        in_cell, in_device = ranks
        for s in range(NP):
            port, block, at = ports_s[s, c], surface_s[s, c], c * NP + s
            this_device = port >> 1
            this_cell = (block >> 3) * 8 + (this_device & 7)
            later = order > at
            in_cell += jnp.where(later & (cell == this_cell), 1, 0)
            in_device += jnp.where(later & (device == this_device), 1, 0)
        return in_cell, in_device

    zero = jnp.zeros((NP, CD), I32)
    in_cell, in_device = lax.fori_loop(0, CD, count, (zero, zero))
    code = 2048 + (ports & 1) * 1024 + (shard * 2 + in_cell) * 64 + order
    here = alive & (owner == me_port)
    code = jnp.where(here, code, 0)
    device_key = target * 2 + in_device
    row = comp * NBL + (surface & 7)
    cell_key = jnp.where(shard == me_port, owner * 2 + in_cell, -1)
    q = lax.broadcasted_iota(I32, (TOP, CD), 0)
    wanted = (q >> 3) * 2 + (q & 1)
    total = jnp.zeros((TOP, CD), I32)
    for s in range(NP):
        total += jnp.where(device_key[s : s + 1] == wanted, code[s : s + 1], 0)
    table[0:TOP] = jnp.broadcast_to(jnp.sum(total, axis=1, keepdims=True), (TOP, 128))
    wanted = lax.broadcasted_iota(I32, (16, CD), 0)
    total = jnp.zeros((16, CD), I32)
    for s in range(NP):
        total += jnp.where(cell_key[s : s + 1] == wanted, row[s : s + 1], 0)
    table[TOP : TOP + 16] = jnp.broadcast_to(jnp.sum(total, axis=1, keepdims=True), (16, 128))


def kernel(
    offs,
    ports_s,
    surface_s,
    ports_v,
    surface_v,
    counts_v,
    shapes,
    values,
    cond_hbm,
    cap_hbm,
    coupling,
    boundary,
    sums_out,
    face_out,
    phi,
    phi_t,
    vals,
    coup,
    cond,
    cap,
    bound,
    table,
    table_s,
    codes,
    codes_s,
    rows_out,
    rows_in,
    halo_lo,
    halo_hi,
    win,
    scaled,
    part,
    pair_in,
    zsum,
    z_in,
    fac_out,
    fac_in,
    late_out,
    late_in,
    both,
    acc,
    load_sem,
    vals_sem,
    rows_ss,
    rows_rs,
    halo_ss,
    halo_rs,
    pair_ss,
    pair_rs,
    z_ss,
    z_rs,
    fac_ss,
    fac_rs,
    code_ss,
    code_rs,
    late_ss,
    late_rs,
):
    c_me, p_me = lax.axis_index("comp"), lax.axis_index("port")
    y, x = c_me // 4, c_me % 4
    z, core = p_me // 2, p_me % 2
    before, after = (p_me + PORTS - 1) % PORTS, (p_me + 1) % PORTS

    def to_comp(hop):
        return ((y + hop[0]) % 4) * 4 + (x + hop[1]) % 4

    def from_comp(hop):
        return ((y + 4 - hop[0]) % 4) * 4 + (x + 4 - hop[1]) % 4

    barrier = pltpu.get_barrier_semaphore()

    @pl.loop(1, PORTS)
    def _(j):
        pl.semaphore_signal(barrier, 1, device_id={"port": (p_me + j) % PORTS}, device_id_type=pl.DeviceIdType.MESH)

    for hop in HOPS:
        pl.semaphore_signal(barrier, 1, device_id={"comp": to_comp(hop)}, device_id_type=pl.DeviceIdType.MESH)

    load_phi = pltpu.make_async_copy(shapes, phi, load_sem.at[0])
    load_coup = pltpu.make_async_copy(coupling, coup, load_sem.at[1])
    load_cond = pltpu.make_async_copy(cond_hbm, cond, load_sem.at[2])
    load_cap = pltpu.make_async_copy(cap_hbm, cap, load_sem.at[3])
    load_bound = pltpu.make_async_copy(boundary, bound, load_sem.at[4])
    load_phi.start()
    load_coup.start()
    load_cond.start()
    load_cap.start()

    def load_vals(c):
        return pltpu.make_async_copy(values.at[c], vals.at[c], vals_sem.at[c])

    @pl.loop(0, CD)
    def _(c):
        load_vals(c).start()

    load_bound.start()
    fill_tables(p_me, ports_s, surface_s, ports_v, surface_v, counts_v, table)
    to_smem = pltpu.make_async_copy(table, table_s, load_sem.at[5])
    to_smem.start()
    load_phi.wait()
    to_smem.wait()

    @pl.loop(0, PORTS)
    def _(o):
        for k in range(2):
            picked = table_s[TOP + 2 * o + k, 0]
            rows_out[o, k] = phi[picked].T

    load_coup.wait()
    for hop in HOPS[:EARLY]:
        d = to_comp(hop)
        for k in range(2):
            fac_out[d, pl.ds(k * M, M)] = coup[table_s[d * 8 + k, 0] & 63]

    rows_in[p_me] = rows_out[p_me]
    codes[pl.ds(pl.multiple_of(c_me * 8, 8), 8)] = table[pl.ds(pl.multiple_of(c_me * 8, 8), 8)]
    pl.semaphore_wait(barrier, PORTS - 1 + COMPS - 1)

    def send_rows(j):
        o = (p_me + j) % PORTS
        return remote(rows_out.at[o], rows_in.at[p_me], rows_ss.at[o], rows_rs.at[p_me], port=o)

    def recv_rows(j):
        o = (p_me + PORTS - j) % PORTS
        return remote(rows_out.at[o], rows_in.at[o], rows_ss.at[o], rows_rs.at[o], port=o)

    for j in Z_HOPS:
        send_rows(j).start()

    def send_codes(hop):
        d = to_comp(hop)
        return remote(
            table.at[pl.ds(pl.multiple_of(d * 8, 8), 8)],
            codes.at[pl.ds(pl.multiple_of(c_me * 8, 8), 8)],
            code_ss.at[d],
            code_rs.at[c_me],
            comp=d,
        )

    def recv_codes(hop):
        d = from_comp(hop)
        return remote(
            table.at[pl.ds(pl.multiple_of(d * 8, 8), 8)],
            codes.at[pl.ds(pl.multiple_of(d * 8, 8), 8)],
            code_ss.at[d],
            code_rs.at[d],
            comp=d,
        )

    def send_factors(hop):
        d = to_comp(hop)
        return remote(fac_out.at[d], fac_in.at[c_me], fac_ss.at[d], fac_rs.at[c_me], comp=d)

    def recv_factors(hop):
        d = from_comp(hop)
        return remote(fac_out.at[d], fac_in.at[d], fac_ss.at[d], fac_rs.at[d], comp=d)

    def send_late(hop):
        d = to_comp(hop)
        return remote(late_out.at[d], late_in.at[c_me], late_ss.at[d], late_rs.at[c_me], comp=d)

    def recv_late(hop):
        d = from_comp(hop)
        return remote(late_out.at[d], late_in.at[d], late_ss.at[d], late_rs.at[d], comp=d)

    for hop in HOPS[:EARLY]:
        send_factors(hop).start()
    for hop in HOPS:
        send_codes(hop).start()

    def send_up(c):
        return remote(
            shapes.at[pl.ds(c * NBL + NBL - 2, 2)], halo_lo.at[c], halo_ss.at[0, c], halo_rs.at[0, c], port=after
        )

    def send_down(c):
        return remote(shapes.at[pl.ds(c * NBL, 2)], halo_hi.at[c], halo_ss.at[1, c], halo_rs.at[1, c], port=before)

    @pl.loop(0, CD)
    def _(c):
        send_up(c).start()
        send_down(c).start()

    def inner(c):
        load_vals(c).wait()
        for r in range(NBL):
            phi_t[c * NBL + r] = phi[c * NBL + r].T
        cond_row, cap_row = row_of_cells(cond, c), row_of_cells(cap, c)
        for r in range(NBL):
            cells = slice(r * BS, (r + 1) * BS)
            own = phi_t[c * NBL + r].astype(F32)
            scaled[c, M : 2 * M, cells] = (cap_row[:, cells] * own).astype(BF)
            if 2 <= r < NBL - 2:
                near = jnp.concatenate([phi_t[c * NBL + r + offs[k, r, c]] for k in range(NB)], axis=1)
                scaled[c, 0:M, cells] = block_row(c, r, near, own, cond_row)

    def row_of_cells(source, c):
        mine = lax.broadcasted_iota(I32, (8, NBL * BS), 0) == c % 8
        return jnp.sum(jnp.where(mine, source[pl.ds(pl.multiple_of((c // 8) * 8, 8), 8)], 0.0), axis=0, keepdims=True)

    def block_row(c, r, near, own, cond_row):
        blocks = jnp.concatenate([vals[c, r, k] for k in range(NB)], axis=1)
        return (nt(near, blocks) + cond_row[:, r * BS : (r + 1) * BS] * own).astype(BF)

    load_cond.wait()
    load_cap.wait()
    pl.loop(0, AHEAD)(inner)

    @pl.loop(1, PORTS)
    def _(j):
        recv_rows(j).wait_recv()

    def row_of(code):
        return rows_in[(code >> 7) & 7, (code >> 6) & 1]

    def factor(d, k):
        code = table_s[d * 8 + k, 0]
        return jnp.dot(row_of(code), coup[code & 63], preferred_element_type=F32).astype(BF)

    for hop in HOPS[:EARLY]:
        d = to_comp(hop)
        for k in range(2):
            late_out[d, k] = row_of(table_s[d * 8 + k, 0])
        send_late(hop).start()
    for hop in HOPS[EARLY:]:
        d = to_comp(hop)
        for k in range(2):
            fac_out[d, pl.ds(k * M, M)] = factor(d, k)
        send_factors(hop).start()

    for k in range(2):
        fac_in[c_me, pl.ds(k * M, M)] = factor(c_me, k)

    def send_pair(c):
        return remote(
            part.at[1 - core, :, c], pair_in.at[:, c], pair_ss.at[c], pair_rs.at[c], port=2 * z + 1 - core
        )

    def send_z(d, h):
        to = (z + d) % 4
        return remote(
            zsum.at[to, pl.ds(2 * h, 2)], z_in.at[z, pl.ds(2 * h, 2)], z_ss.at[to, h], z_rs.at[z, h], port=2 * to + core
        )

    def recv_z(d, h):
        at = (z + 4 - d) % 4
        return remote(
            zsum.at[at, pl.ds(2 * h, 2)], z_in.at[at, pl.ds(2 * h, 2)], z_ss.at[at, h], z_rs.at[at, h], port=2 * at + core
        )

    def chip_sums(h):
        for i in range(2):
            c = 2 * h + i
            send_pair(c).wait_recv()
            zsum[:, c] = part[core, :, c] + pair_in[:, c]
        for d in range(1, 4):
            send_z(d, h).start()

    first = jnp.where(p_me == 0, 0.0, 1.0)
    last = jnp.where(p_me == PORTS - 1, 0.0, 1.0)

    def modal(c):
        send_up(c).wait_recv()
        send_down(c).wait_recv()
        for i in range(2):
            win[i] = (halo_lo[c, i].astype(F32) * first).T.astype(BF)
            win[NBL + 2 + i] = (halo_hi[c, i].astype(F32) * last).T.astype(BF)
        for r in range(NBL):
            win[2 + r] = phi_t[c * NBL + r]
        cond_row = row_of_cells(cond, c)
        for r in (0, 1, NBL - 2, NBL - 1):
            near = jnp.concatenate([win[r + 2 + offs[k, r, c]] for k in range(NB)], axis=1)
            scaled[c, 0:M, r * BS : (r + 1) * BS] = block_row(c, r, near, win[r + 2].astype(F32), cond_row)
        every = jnp.concatenate([phi_t[c * NBL + r] for r in range(NBL)], axis=1)
        sums = nt(every, scaled[c])
        for p in range(PORTS):
            part[p % 2, p // 2, c] = sums[16 * p : 16 * p + 16]

    pl.loop(AHEAD, CD)(inner)

    @pl.loop(0, CD // 2)
    def _(h):
        @pl.loop(0, 2)
        def _(i):
            modal(2 * h + i)
            send_pair(2 * h + i).start()

        @pl.when(h > 0)
        def _():
            chip_sums(h - 1)

    chip_sums(CD // 2 - 1)

    def gather_sums():
        @pl.loop(0, CD // 2)
        def _(h):
            for d in range(1, 4):
                recv_z(d, h).wait_recv()
            for i in range(2):
                c = 2 * h + i
                total = zsum[z, c]
                for d in range(1, 4):
                    total = total + z_in[(z + 4 - d) % 4, c]
                sums_out[c] = total
            for d in range(1, 4):
                send_z(d, h).wait_send()

    for hop in HOPS:
        recv_codes(hop).wait_recv()
    to_smem = pltpu.make_async_copy(codes, codes_s, load_sem.at[6])
    to_smem.start()
    acc[...] = jnp.zeros_like(acc)
    to_smem.wait()

    def square(d, factors):
        for o in range(2):
            halves = []
            for k in range(2):
                code = codes_s[d * 8 + k, 0]
                weight = jnp.where((code >> 10) == 2 + o, 1.0, 0.0).astype(F32)
                halves.append((factors[pl.ds(k * M, M)].astype(F32) * weight).astype(BF))
            acc[o] += tn(jnp.concatenate(halves, axis=0), factors[...])

    square(c_me, fac_in.at[c_me])
    for hop in HOPS[:EARLY]:
        d = from_comp(hop)
        recv_factors(hop).wait_recv()
        recv_late(hop).wait_recv()
        for k in range(2):
            half = pl.ds(k * M, M)
            both[half] = jnp.dot(late_in[d, k], fac_in[d, half], preferred_element_type=F32).astype(BF)
        square(d, both)
    for at, hop in enumerate(HOPS[EARLY:]):
        if at == len(HOPS) - EARLY - LAST:
            gather_sums()
        recv_factors(hop).wait_recv()
        square(from_comp(hop), fac_in.at[from_comp(hop)])

    load_bound.wait()
    face_out[...] = bound[...] + acc[...] * (1.0 / M)

    @pl.loop(0, CD)
    def _(c):
        send_up(c).wait_send()
        send_down(c).wait_send()
        send_pair(c).wait_send()

    @pl.loop(1, PORTS)
    def _(j):
        send_rows(j).wait_send()

    for hop in HOPS:
        send_factors(hop).wait_send()
        send_codes(hop).wait_send()
    for hop in HOPS[:EARLY]:
        send_late(hop).wait_send()


def finish(sums, face, cond_out, cap_out, face_out):
    cond_out[...] = sums[:, :, 0:M]
    cap_out[...] = sums[:, :, M : 2 * M]
    face_out[...] = face[...]


def shards(
    mode_shapes,
    block_values,
    block_offsets,
    conductance,
    capacity,
    coupling,
    surface_blocks,
    port_ids,
    port_counts,
    boundary,
):
    smem = pl.BlockSpec(memory_space=pltpu.SMEM)
    vmem = pl.BlockSpec(memory_space=pltpu.VMEM)
    hbm = pl.BlockSpec(memory_space=pltpu.HBM)
    dma = pltpu.SemaphoreType.DMA
    ports, surface = port_ids.T, surface_blocks.T
    modal = jax.ShapeDtypeStruct((CD, M // PORTS, M), F32)
    sums, face = pl.pallas_call(
        kernel,
        out_shape=(
            pltpu.VMEM((CD, M // PORTS, 2 * M), F32),
            pltpu.VMEM((2, PB, PB), F32),
        ),
        in_specs=[smem] * 3 + [vmem] * 3 + [hbm] * 6,
        out_specs=(vmem, vmem),
        scratch_shapes=[
            pltpu.VMEM((CD * NBL, BS, M), BF),
            pltpu.VMEM((CD * NBL, M, BS), BF),
            pltpu.VMEM((CD, NBL, NB, BS, BS), BF),
            pltpu.VMEM((CD * NP, BS, PB), BF),
            pltpu.VMEM((CD, NBL * BS), F32),
            pltpu.VMEM((CD, NBL * BS), F32),
            pltpu.VMEM((2, PB, PB), F32),
            pltpu.VMEM((TOP + 16, 128), I32),
            pltpu.SMEM((TOP + 16, 128), I32),
            pltpu.VMEM((TOP, 128), I32),
            pltpu.SMEM((TOP, 128), I32),
            pltpu.VMEM((PORTS, 2, M, BS), BF),
            pltpu.VMEM((PORTS, 2, M, BS), BF),
            pltpu.VMEM((CD, 2, BS, M), BF),
            pltpu.VMEM((CD, 2, BS, M), BF),
            pltpu.VMEM((NBL + 4, M, BS), BF),
            pltpu.VMEM((CD, 2 * M, NBL * BS), BF),
            pltpu.VMEM((2, 4, CD, 16, 2 * M), F32),
            pltpu.VMEM((4, CD, 16, 2 * M), F32),
            pltpu.VMEM((4, CD, 16, 2 * M), F32),
            pltpu.VMEM((4, CD, 16, 2 * M), F32),
            pltpu.VMEM((COMPS, 2 * M, PB), BF),
            pltpu.VMEM((COMPS, 2 * M, PB), BF),
            pltpu.VMEM((COMPS, 2, M, BS), BF),
            pltpu.VMEM((COMPS, 2, M, BS), BF),
            pltpu.VMEM((2 * M, PB), BF),
            pltpu.VMEM((2, PB, PB), F32),
            dma((7,)),
            dma((CD,)),
            dma((PORTS,)),
            dma((PORTS,)),
            dma((2, CD)),
            dma((2, CD)),
            dma((CD,)),
            dma((CD,)),
            dma((4, CD // 2)),
            dma((4, CD // 2)),
            dma((COMPS,)),
            dma((COMPS,)),
            dma((COMPS,)),
            dma((COMPS,)),
            dma((COMPS,)),
            dma((COMPS,)),
        ],
        compiler_params=pltpu.CompilerParams(
            collective_id=0, has_side_effects=True, vmem_limit_bytes=62 << 20
        ),
        name="reduce_components",
    )(
        block_offsets.transpose(2, 1, 0),
        ports,
        surface,
        ports,
        surface,
        port_counts.reshape(1, CD),
        mode_shapes.reshape(CD * NBL, BS, M),
        block_values,
        conductance,
        capacity,
        coupling.reshape(CD * NP, BS, PB),
        boundary,
    )
    return pl.pallas_call(
        finish,
        out_shape=(modal, modal, jax.ShapeDtypeStruct((2, PB, PB), F32)),
        in_specs=[vmem, vmem],
        out_specs=(vmem, vmem, vmem),
        compiler_params=pltpu.CompilerParams(vmem_limit_bytes=62 << 20),
        name="finish",
    )(pltpu.with_memory_space_constraint(sums, pltpu.VMEM), pltpu.with_memory_space_constraint(face, pltpu.VMEM))


def solution(mesh):
    in_specs = (
        P("comp", "port", None),
        P("comp", "port", None, None, None),
        P("comp", "port", None),
        P("comp", "port"),
        P("comp", "port"),
        P("comp", None, None, None),
        P("comp", None),
        P("comp", None),
        P("comp"),
        P(("comp", "port"), None, None),
    )
    out_specs = (P("comp", "port", None), P("comp", "port", None), P(("comp", "port"), None, None))
    return jax.shard_map(shards, mesh=mesh, in_specs=in_specs, out_specs=out_specs, check_vma=False)
```

```python
import jax
import jax.numpy as jnp
from jax import lax
from jax.experimental import pallas as pl
from jax.experimental.pallas import tpu as pltpu
from jax.sharding import PartitionSpec as P

BF, F32, I32 = jnp.bfloat16, jnp.float32, jnp.int32
COMPS, PORTS = 16, 8
CD, NBL, NB, NP = 16, 8, 3, 4
BS, M, PB = 128, 128, 256
HOPS = ((0, 1), (0, 3), (1, 0), (3, 0), (1, 1), (3, 3), (1, 3), (3, 1), (2, 0), (0, 2), (2, 3), (2, 1), (3, 2), (1, 2), (2, 2))
EARLY = 10
LAST = 3
AHEAD = 12
Z_HOPS = (4, 5, 2, 3, 6, 7, 1)
TOP = COMPS * 8


def nt(a, b):
    return lax.dot_general(a, b, (((1,), (1,)), ((), ())), preferred_element_type=F32)


def tn(a, b):
    return lax.dot_general(a, b, (((0,), (0,)), ((), ())), preferred_element_type=F32)


def remote(src, dst, send, recv, **where):
    return pltpu.make_async_remote_copy(
        src_ref=src,
        dst_ref=dst,
        send_sem=send,
        recv_sem=recv,
        device_id=where,
        device_id_type=pl.DeviceIdType.MESH,
    )


def fill_tables(me_port, ports_s, surface_s, ports_v, surface_v, counts_v, table):
    ports, surface = ports_v[...], surface_v[...]
    owner, target = (ports >> 1) & 7, ports >> 4
    shard = surface >> 3
    cell, device = shard * 8 + owner, ports >> 1
    comp = lax.broadcasted_iota(I32, (NP, CD), 1)
    slot = lax.broadcasted_iota(I32, (NP, CD), 0)
    order = comp * NP + slot
    alive = slot < counts_v[...]

    def count(c, ranks):
        in_cell, in_device = ranks
        for s in range(NP):
            port, block, at = ports_s[s, c], surface_s[s, c], c * NP + s
            this_device = port >> 1
            this_cell = (block >> 3) * 8 + (this_device & 7)
            later = order > at
            in_cell += jnp.where(later & (cell == this_cell), 1, 0)
            in_device += jnp.where(later & (device == this_device), 1, 0)
        return in_cell, in_device

    zero = jnp.zeros((NP, CD), I32)
    in_cell, in_device = lax.fori_loop(0, CD, count, (zero, zero))
    code = 2048 + (ports & 1) * 1024 + (shard * 2 + in_cell) * 64 + order
    here = alive & (owner == me_port)
    code = jnp.where(here, code, 0)
    device_key = target * 2 + in_device
    row = comp * NBL + (surface & 7)
    cell_key = jnp.where(shard == me_port, owner * 2 + in_cell, -1)
    q = lax.broadcasted_iota(I32, (TOP, CD), 0)
    wanted = (q >> 3) * 2 + (q & 1)
    total = jnp.zeros((TOP, CD), I32)
    for s in range(NP):
        total += jnp.where(device_key[s : s + 1] == wanted, code[s : s + 1], 0)
    table[0:TOP] = jnp.broadcast_to(jnp.sum(total, axis=1, keepdims=True), (TOP, 128))
    wanted = lax.broadcasted_iota(I32, (16, CD), 0)
    total = jnp.zeros((16, CD), I32)
    for s in range(NP):
        total += jnp.where(cell_key[s : s + 1] == wanted, row[s : s + 1], 0)
    table[TOP : TOP + 16] = jnp.broadcast_to(jnp.sum(total, axis=1, keepdims=True), (16, 128))


def kernel(
    offs,
    ports_s,
    surface_s,
    ports_v,
    surface_v,
    counts_v,
    shapes,
    values,
    cond_hbm,
    cap_hbm,
    coupling,
    boundary,
    sums_out,
    face_out,
    phi,
    phi_t,
    vals,
    coup,
    cond,
    cap,
    bound,
    table,
    table_s,
    codes,
    codes_s,
    rows_out,
    rows_in,
    halo_lo,
    halo_hi,
    win,
    scaled,
    part,
    pair_in,
    zsum,
    z_in,
    fac_out,
    fac_in,
    late_out,
    late_in,
    both,
    acc,
    load_sem,
    vals_sem,
    rows_ss,
    rows_rs,
    halo_ss,
    halo_rs,
    pair_ss,
    pair_rs,
    z_ss,
    z_rs,
    fac_ss,
    fac_rs,
    code_ss,
    code_rs,
    late_ss,
    late_rs,
):
    c_me, p_me = lax.axis_index("comp"), lax.axis_index("port")
    y, x = c_me // 4, c_me % 4
    z, core = p_me // 2, p_me % 2
    before, after = (p_me + PORTS - 1) % PORTS, (p_me + 1) % PORTS

    def to_comp(hop):
        return ((y + hop[0]) % 4) * 4 + (x + hop[1]) % 4

    def from_comp(hop):
        return ((y + 4 - hop[0]) % 4) * 4 + (x + 4 - hop[1]) % 4

    barrier = pltpu.get_barrier_semaphore()

    @pl.loop(1, PORTS)
    def _(j):
        pl.semaphore_signal(barrier, 1, device_id={"port": (p_me + j) % PORTS}, device_id_type=pl.DeviceIdType.MESH)

    for hop in HOPS:
        pl.semaphore_signal(barrier, 1, device_id={"comp": to_comp(hop)}, device_id_type=pl.DeviceIdType.MESH)

    load_phi = pltpu.make_async_copy(shapes, phi, load_sem.at[0])
    load_coup = pltpu.make_async_copy(coupling, coup, load_sem.at[1])
    load_cond = pltpu.make_async_copy(cond_hbm, cond, load_sem.at[2])
    load_cap = pltpu.make_async_copy(cap_hbm, cap, load_sem.at[3])
    load_bound = pltpu.make_async_copy(boundary, bound, load_sem.at[4])
    load_phi.start()
    load_coup.start()
    load_cond.start()
    load_cap.start()

    def load_vals(c):
        return pltpu.make_async_copy(values.at[c], vals.at[c], vals_sem.at[c])

    @pl.loop(0, CD)
    def _(c):
        load_vals(c).start()

    load_bound.start()
    fill_tables(p_me, ports_s, surface_s, ports_v, surface_v, counts_v, table)
    to_smem = pltpu.make_async_copy(table, table_s, load_sem.at[5])
    to_smem.start()
    load_phi.wait()
    to_smem.wait()

    @pl.loop(0, PORTS)
    def _(o):
        for k in range(2):
            picked = table_s[TOP + 2 * o + k, 0]
            rows_out[o, k] = phi[picked].T

    load_coup.wait()
    for hop in HOPS[:EARLY]:
        d = to_comp(hop)
        for k in range(2):
            fac_out[d, pl.ds(k * M, M)] = coup[table_s[d * 8 + k, 0] & 63]

    rows_in[p_me] = rows_out[p_me]
    codes[pl.ds(pl.multiple_of(c_me * 8, 8), 8)] = table[pl.ds(pl.multiple_of(c_me * 8, 8), 8)]
    pl.semaphore_wait(barrier, PORTS - 1 + COMPS - 1)

    def send_rows(j):
        o = (p_me + j) % PORTS
        return remote(rows_out.at[o], rows_in.at[p_me], rows_ss.at[o], rows_rs.at[p_me], port=o)

    def recv_rows(j):
        o = (p_me + PORTS - j) % PORTS
        return remote(rows_out.at[o], rows_in.at[o], rows_ss.at[o], rows_rs.at[o], port=o)

    for j in Z_HOPS:
        send_rows(j).start()

    def send_codes(hop):
        d = to_comp(hop)
        return remote(
            table.at[pl.ds(pl.multiple_of(d * 8, 8), 8)],
            codes.at[pl.ds(pl.multiple_of(c_me * 8, 8), 8)],
            code_ss.at[d],
            code_rs.at[c_me],
            comp=d,
        )

    def recv_codes(hop):
        d = from_comp(hop)
        return remote(
            table.at[pl.ds(pl.multiple_of(d * 8, 8), 8)],
            codes.at[pl.ds(pl.multiple_of(d * 8, 8), 8)],
            code_ss.at[d],
            code_rs.at[d],
            comp=d,
        )

    def send_factors(hop):
        d = to_comp(hop)
        return remote(fac_out.at[d], fac_in.at[c_me], fac_ss.at[d], fac_rs.at[c_me], comp=d)

    def recv_factors(hop):
        d = from_comp(hop)
        return remote(fac_out.at[d], fac_in.at[d], fac_ss.at[d], fac_rs.at[d], comp=d)

    def send_late(hop):
        d = to_comp(hop)
        return remote(late_out.at[d], late_in.at[c_me], late_ss.at[d], late_rs.at[c_me], comp=d)

    def recv_late(hop):
        d = from_comp(hop)
        return remote(late_out.at[d], late_in.at[d], late_ss.at[d], late_rs.at[d], comp=d)

    for hop in HOPS[:EARLY]:
        send_factors(hop).start()
    for hop in HOPS:
        send_codes(hop).start()

    def send_up(c):
        return remote(
            shapes.at[pl.ds(c * NBL + NBL - 2, 2)], halo_lo.at[c], halo_ss.at[0, c], halo_rs.at[0, c], port=after
        )

    def send_down(c):
        return remote(shapes.at[pl.ds(c * NBL, 2)], halo_hi.at[c], halo_ss.at[1, c], halo_rs.at[1, c], port=before)

    def inner(c):
        load_vals(c).wait()
        for r in range(NBL):
            phi_t[c * NBL + r] = phi[c * NBL + r].T
        cond_row, cap_row = row_of_cells(cond, c), row_of_cells(cap, c)
        for r in range(NBL):
            cells = slice(r * BS, (r + 1) * BS)
            own = phi_t[c * NBL + r].astype(F32)
            scaled[c, M : 2 * M, cells] = (cap_row[:, cells] * own).astype(BF)
            if 2 <= r < NBL - 2:
                near = jnp.concatenate([phi_t[c * NBL + r + offs[k, r, c]] for k in range(NB)], axis=1)
                scaled[c, 0:M, cells] = block_row(c, r, near, own, cond_row)

    def row_of_cells(source, c):
        mine = lax.broadcasted_iota(I32, (8, NBL * BS), 0) == c % 8
        return jnp.sum(jnp.where(mine, source[pl.ds(pl.multiple_of((c // 8) * 8, 8), 8)], 0.0), axis=0, keepdims=True)

    def block_row(c, r, near, own, cond_row):
        blocks = jnp.concatenate([vals[c, r, k] for k in range(NB)], axis=1)
        return (nt(near, blocks) + cond_row[:, r * BS : (r + 1) * BS] * own).astype(BF)

    load_cond.wait()
    load_cap.wait()
    pl.loop(0, 4)(inner)

    @pl.loop(0, CD)
    def _(c):
        send_up(c).start()
        send_down(c).start()

    pl.loop(4, AHEAD)(inner)

    @pl.loop(1, PORTS)
    def _(j):
        recv_rows(j).wait_recv()

    def row_of(code):
        return rows_in[(code >> 7) & 7, (code >> 6) & 1]

    def factor(d, k):
        code = table_s[d * 8 + k, 0]
        return jnp.dot(row_of(code), coup[code & 63], preferred_element_type=F32).astype(BF)

    for hop in HOPS[:EARLY]:
        d = to_comp(hop)
        for k in range(2):
            late_out[d, k] = row_of(table_s[d * 8 + k, 0])
        send_late(hop).start()
    for hop in HOPS[EARLY:]:
        d = to_comp(hop)
        for k in range(2):
            fac_out[d, pl.ds(k * M, M)] = factor(d, k)
        send_factors(hop).start()

    for k in range(2):
        fac_in[c_me, pl.ds(k * M, M)] = factor(c_me, k)

    def send_pair(c):
        return remote(
            part.at[1 - core, :, c], pair_in.at[:, c], pair_ss.at[c], pair_rs.at[c], port=2 * z + 1 - core
        )

    def send_z(d, h):
        to = (z + d) % 4
        return remote(
            zsum.at[to, pl.ds(2 * h, 2)], z_in.at[z, pl.ds(2 * h, 2)], z_ss.at[to, h], z_rs.at[z, h], port=2 * to + core
        )

    def recv_z(d, h):
        at = (z + 4 - d) % 4
        return remote(
            zsum.at[at, pl.ds(2 * h, 2)], z_in.at[at, pl.ds(2 * h, 2)], z_ss.at[at, h], z_rs.at[at, h], port=2 * at + core
        )

    def chip_sums(h):
        for i in range(2):
            c = 2 * h + i
            send_pair(c).wait_recv()
            zsum[:, c] = part[core, :, c] + pair_in[:, c]
        for d in range(1, 4):
            send_z(d, h).start()

    first = jnp.where(p_me == 0, 0.0, 1.0)
    last = jnp.where(p_me == PORTS - 1, 0.0, 1.0)

    def modal(c):
        send_up(c).wait_recv()
        send_down(c).wait_recv()
        for i in range(2):
            win[i] = (halo_lo[c, i].astype(F32) * first).T.astype(BF)
            win[NBL + 2 + i] = (halo_hi[c, i].astype(F32) * last).T.astype(BF)
        for r in range(NBL):
            win[2 + r] = phi_t[c * NBL + r]
        cond_row = row_of_cells(cond, c)
        for r in (0, 1, NBL - 2, NBL - 1):
            near = jnp.concatenate([win[r + 2 + offs[k, r, c]] for k in range(NB)], axis=1)
            scaled[c, 0:M, r * BS : (r + 1) * BS] = block_row(c, r, near, win[r + 2].astype(F32), cond_row)
        every = jnp.concatenate([phi_t[c * NBL + r] for r in range(NBL)], axis=1)
        sums = nt(every, scaled[c])
        for p in range(PORTS):
            part[p % 2, p // 2, c] = sums[16 * p : 16 * p + 16]

    pl.loop(AHEAD, CD)(inner)

    @pl.loop(0, CD // 2)
    def _(h):
        @pl.loop(0, 2)
        def _(i):
            modal(2 * h + i)
            send_pair(2 * h + i).start()

        @pl.when(h > 0)
        def _():
            chip_sums(h - 1)

    chip_sums(CD // 2 - 1)

    def gather_sums():
        @pl.loop(0, CD // 2)
        def _(h):
            for d in range(1, 4):
                recv_z(d, h).wait_recv()
            for i in range(2):
                c = 2 * h + i
                total = zsum[z, c]
                for d in range(1, 4):
                    total = total + z_in[(z + 4 - d) % 4, c]
                sums_out[c] = total
            for d in range(1, 4):
                send_z(d, h).wait_send()

    for hop in HOPS:
        recv_codes(hop).wait_recv()
    to_smem = pltpu.make_async_copy(codes, codes_s, load_sem.at[6])
    to_smem.start()
    acc[...] = jnp.zeros_like(acc)
    to_smem.wait()

    def square(d, factors):
        for o in range(2):
            halves = []
            for k in range(2):
                code = codes_s[d * 8 + k, 0]
                weight = jnp.where((code >> 10) == 2 + o, 1.0, 0.0).astype(F32)
                halves.append((factors[pl.ds(k * M, M)].astype(F32) * weight).astype(BF))
            acc[o] += tn(jnp.concatenate(halves, axis=0), factors[...])

    square(c_me, fac_in.at[c_me])
    for hop in HOPS[:EARLY]:
        d = from_comp(hop)
        recv_factors(hop).wait_recv()
        recv_late(hop).wait_recv()
        for k in range(2):
            half = pl.ds(k * M, M)
            both[half] = jnp.dot(late_in[d, k], fac_in[d, half], preferred_element_type=F32).astype(BF)
        square(d, both)
    for at, hop in enumerate(HOPS[EARLY:]):
        if at == len(HOPS) - EARLY - LAST:
            gather_sums()
        recv_factors(hop).wait_recv()
        square(from_comp(hop), fac_in.at[from_comp(hop)])

    load_bound.wait()
    face_out[...] = bound[...] + acc[...] * (1.0 / M)

    @pl.loop(0, CD)
    def _(c):
        send_up(c).wait_send()
        send_down(c).wait_send()
        send_pair(c).wait_send()

    @pl.loop(1, PORTS)
    def _(j):
        send_rows(j).wait_send()

    for hop in HOPS:
        send_factors(hop).wait_send()
        send_codes(hop).wait_send()
    for hop in HOPS[:EARLY]:
        send_late(hop).wait_send()


def finish(sums, face, cond_out, cap_out, face_out):
    cond_out[...] = sums[:, :, 0:M]
    cap_out[...] = sums[:, :, M : 2 * M]
    face_out[...] = face[...]


def shards(
    mode_shapes,
    block_values,
    block_offsets,
    conductance,
    capacity,
    coupling,
    surface_blocks,
    port_ids,
    port_counts,
    boundary,
):
    smem = pl.BlockSpec(memory_space=pltpu.SMEM)
    vmem = pl.BlockSpec(memory_space=pltpu.VMEM)
    hbm = pl.BlockSpec(memory_space=pltpu.HBM)
    dma = pltpu.SemaphoreType.DMA
    ports, surface = port_ids.T, surface_blocks.T
    modal = jax.ShapeDtypeStruct((CD, M // PORTS, M), F32)
    sums, face = pl.pallas_call(
        kernel,
        out_shape=(
            pltpu.VMEM((CD, M // PORTS, 2 * M), F32),
            pltpu.VMEM((2, PB, PB), F32),
        ),
        in_specs=[smem] * 3 + [vmem] * 3 + [hbm] * 6,
        out_specs=(vmem, vmem),
        scratch_shapes=[
            pltpu.VMEM((CD * NBL, BS, M), BF),
            pltpu.VMEM((CD * NBL, M, BS), BF),
            pltpu.VMEM((CD, NBL, NB, BS, BS), BF),
            pltpu.VMEM((CD * NP, BS, PB), BF),
            pltpu.VMEM((CD, NBL * BS), F32),
            pltpu.VMEM((CD, NBL * BS), F32),
            pltpu.VMEM((2, PB, PB), F32),
            pltpu.VMEM((TOP + 16, 128), I32),
            pltpu.SMEM((TOP + 16, 128), I32),
            pltpu.VMEM((TOP, 128), I32),
            pltpu.SMEM((TOP, 128), I32),
            pltpu.VMEM((PORTS, 2, M, BS), BF),
            pltpu.VMEM((PORTS, 2, M, BS), BF),
            pltpu.VMEM((CD, 2, BS, M), BF),
            pltpu.VMEM((CD, 2, BS, M), BF),
            pltpu.VMEM((NBL + 4, M, BS), BF),
            pltpu.VMEM((CD, 2 * M, NBL * BS), BF),
            pltpu.VMEM((2, 4, CD, 16, 2 * M), F32),
            pltpu.VMEM((4, CD, 16, 2 * M), F32),
            pltpu.VMEM((4, CD, 16, 2 * M), F32),
            pltpu.VMEM((4, CD, 16, 2 * M), F32),
            pltpu.VMEM((COMPS, 2 * M, PB), BF),
            pltpu.VMEM((COMPS, 2 * M, PB), BF),
            pltpu.VMEM((COMPS, 2, M, BS), BF),
            pltpu.VMEM((COMPS, 2, M, BS), BF),
            pltpu.VMEM((2 * M, PB), BF),
            pltpu.VMEM((2, PB, PB), F32),
            dma((7,)),
            dma((CD,)),
            dma((PORTS,)),
            dma((PORTS,)),
            dma((2, CD)),
            dma((2, CD)),
            dma((CD,)),
            dma((CD,)),
            dma((4, CD // 2)),
            dma((4, CD // 2)),
            dma((COMPS,)),
            dma((COMPS,)),
            dma((COMPS,)),
            dma((COMPS,)),
            dma((COMPS,)),
            dma((COMPS,)),
        ],
        compiler_params=pltpu.CompilerParams(
            collective_id=0, has_side_effects=True, vmem_limit_bytes=62 << 20
        ),
        name="reduce_components",
    )(
        block_offsets.transpose(2, 1, 0),
        ports,
        surface,
        ports,
        surface,
        port_counts.reshape(1, CD),
        mode_shapes.reshape(CD * NBL, BS, M),
        block_values,
        conductance,
        capacity,
        coupling.reshape(CD * NP, BS, PB),
        boundary,
    )
    return pl.pallas_call(
        finish,
        out_shape=(modal, modal, jax.ShapeDtypeStruct((2, PB, PB), F32)),
        in_specs=[vmem, vmem],
        out_specs=(vmem, vmem, vmem),
        compiler_params=pltpu.CompilerParams(vmem_limit_bytes=62 << 20),
        name="finish",
    )(pltpu.with_memory_space_constraint(sums, pltpu.VMEM), pltpu.with_memory_space_constraint(face, pltpu.VMEM))


def solution(mesh):
    in_specs = (
        P("comp", "port", None),
        P("comp", "port", None, None, None),
        P("comp", "port", None),
        P("comp", "port"),
        P("comp", "port"),
        P("comp", None, None, None),
        P("comp", None),
        P("comp", None),
        P("comp"),
        P(("comp", "port"), None, None),
    )
    out_specs = (P("comp", "port", None), P("comp", "port", None), P(("comp", "port"), None, None))
    return jax.shard_map(shards, mesh=mesh, in_specs=in_specs, out_specs=out_specs, check_vma=False)
```
